32 devices in a mesh: clips: 2 (over y), row: 4 (over x, core), col: 4 (over z).
Axes of the slice: x: 2, y: 2, z: 4, core: 2. Of those that a mesh axis runs over, the one named last changes fastest.
Arguments:
- clip_tokens: bfloat16 [2048, 6144], P(('clips', 'col'), 'row'), parts along dimension 0, may hold values from -12 to 12
- modulation: float32 [8, 6, 6144], P('clips', None, 'row'), parts along dimension 0, may hold values from -3 to 3
- w_qkv: bfloat16 [6144, 3, 4096], P('row', None, 'col'), may hold values from -3 to 3
- w_out: bfloat16 [4096, 6144], P('col', 'row'), may hold values from -0.09375 to 0.09375
- w_up: bfloat16 [6144, 12288], P('row', 'col'), may hold values from -0.078125 to 0.078125
- up_bias: float32 [12288], P('col'), may hold values from -3 to 3
- w_down: bfloat16 [12288, 6144], P('col', 'row'), may hold values from -0.0546875 to 0.0546875
- guide_num: int32 [8], P('clips'), parts along dimension 0, may hold values from -3 to 10, as said below
Outputs:
- guided: bfloat16 [512, 6144], P(('clips', 'col'), 'row'), parts along dimension 0
The draws below stay inside these ranges and needn't reach their ends.
There are 2 independent parts, one for each index of `clips`. The reference program is written for one: setup_inputs(seed, part) draws one part's arguments, and reference() takes and returns one part's arrays. A program takes and returns all parts, laid end to end along the dimension named above; an argument that names none is the same for every part. Nothing has to cross between parts.
Inputs may be any that keep to these rules, and one draw needn't show every extreme that they name: `guide_num`: the three negative numerators are -1, -2 and -3 in some order, and the positive one makes the four sum to 4.
All inputs are finite; a program needn't handle non-finite values.
Results may differ from the reference program's by a relative error of at most 0.019.
Values may be sent and summed in bfloat16 or wider, within the bound.
A program may use at most 128 MiB of HBM per device.

```python
import math
import jax
import jax.numpy as jnp
from jax import lax

D = 6144
HEADS = 32
HEAD_DIM = 128
FF = 12288
BRANCHES = 4
SEQ = 256
TOKENS = 1024
INNER = 4096
N_ROW = 4
N_COL = 4


def draw_guide_num(key, part):
    shuffled = jax.random.permutation(key, BRANCHES - 1).astype(jnp.int32) + 1
    positive = 4 + jnp.sum(shuffled)
    return jnp.concatenate([positive[None], -shuffled]).astype(jnp.int32)


def draw_clip_tokens(key, part):
    array_shape = (TOKENS, D)
    position = jnp.arange(D, dtype=jnp.float32) / float(max(D - 1, 1))
    entries = jax.random.truncated_normal(jax.random.fold_in(key, 21), -6.0, 6.0, array_shape, jnp.float32)
    row_scale = jnp.ones((TOKENS, 1), jnp.float32)
    low_end = 0.25
    high_end = 1.5
    rough = jnp.exp(jax.random.uniform(jax.random.fold_in(key, 25), (D,), jnp.float32, math.log(0.75), 0.0))
    column_scale = low_end * jnp.exp(position * math.log(high_end / low_end)) * rough
    copied = jax.random.randint(jax.random.fold_in(key, 23), (TOKENS, 1), 0, 32) == 0
    jitter = 0.15 * jax.random.truncated_normal(jax.random.fold_in(key, 24), -4.0, 4.0, array_shape, jnp.float32)
    earlier = jnp.roll(entries, BRANCHES, axis=0)
    earlier_scale = jnp.roll(row_scale, BRANCHES, axis=0)
    entries = jnp.where(copied, earlier + jitter, entries)
    row_scale = jnp.where(copied, earlier_scale, row_scale)
    return (entries * row_scale * column_scale[None]).astype(jnp.bfloat16)


def draw_w_qkv(key, part):
    array_shape = (D, 3, INNER)
    entries = jax.random.truncated_normal(jax.random.fold_in(key, 11), -4.0, 4.0, array_shape, jnp.float32)
    entries = entries / jnp.sqrt(jnp.float32(D))
    shuffled = jax.random.permutation(jax.random.fold_in(key, 12), HEADS).astype(jnp.int32)
    head_rank = jnp.argsort(shuffled).astype(jnp.int32)
    hot_count = max(HEADS // 8, 1)
    hot_heads = head_rank < hot_count
    spread = head_rank.astype(jnp.float32) / float(max(hot_count - 1, 1))
    factor = jnp.where(hot_heads, 2.6 + 1.6 * spread, 1.0)
    column_factor = jnp.repeat(factor, HEAD_DIM)
    hot_columns = jnp.repeat(hot_heads, HEAD_DIM)
    query_part = entries[:, 0] * column_factor[None]
    key_part = jnp.where(hot_columns[None], query_part, entries[:, 1])
    return jnp.stack([query_part, key_part, entries[:, 2]], axis=1).astype(jnp.bfloat16)


def steps_of(own_key, shape, split, smallest, top_value):
    loudness, own = 1.0, jax.random.fold_in(own_key, 6)
    for dim, parts in split:
        heights = jnp.exp(jax.random.uniform(jax.random.fold_in(own, dim), (parts,), jnp.float32, smallest / len(split), top_value / len(split)))
        loudness = loudness * jnp.repeat(heights, shape[dim] // parts).reshape([-1 if axis == dim else 1 for axis in range(len(shape))])
    return loudness


def centred(own_key, extent, scale, reach, pieces=(), held_as=jnp.bfloat16):
    array = scale * jax.random.normal(own_key, extent, jnp.float32)
    if pieces:
        array = array * steps_of(own_key, extent, pieces, -0.22, 0.18)
    return jnp.clip(array, -reach, reach).astype(held_as)


def setup_inputs(seed: int = 0, part: int = 0) -> dict:
    arg_keys = jax.random.split(jax.random.key(seed), 9)
    own_keys = jax.random.split(jax.random.fold_in(arg_keys[8], part), 9)
    clip_tokens = draw_clip_tokens(jax.random.fold_in(jax.random.fold_in(arg_keys[8], part), 71), part)
    modulation = centred(own_keys[1], (BRANCHES, 6, D), 0.5, 3.0, ((2, 4),), jnp.float32)
    w_qkv = draw_w_qkv(jax.random.fold_in(arg_keys[8], 71), part)
    w_out = centred(arg_keys[3], (INNER, D), INNER ** -0.5, 0.09375, ((0, 4), (1, 4)))
    w_up = centred(arg_keys[4], (D, FF), D ** -0.5, 0.078125, ((0, 4), (1, 4)))
    up_bias = centred(arg_keys[5], (FF,), 0.5, 3.0, ((0, 4),), jnp.float32)
    w_down = centred(arg_keys[6], (FF, D), FF ** -0.5, 0.0546875, ((0, 4), (1, 4)))
    guide_num = draw_guide_num(jax.random.fold_in(jax.random.fold_in(arg_keys[8], part), 71), part)
    return dict(clip_tokens=clip_tokens, modulation=modulation, w_qkv=w_qkv, w_out=w_out, w_up=w_up, up_bias=up_bias, w_down=w_down, guide_num=guide_num)


eps = 1e-06

def normalize(values, shift, scale):
    total = lax.optimization_barrier(jnp.sum(values, axis=1))
    squares = lax.optimization_barrier(jnp.sum(values * values, axis=1))
    mean = total / D
    variance = squares / D - mean * mean
    normed = (values - mean[:, None]) * lax.rsqrt(variance + eps)[:, None]
    shaped = normed.reshape(-1, BRANCHES, values.shape[1]) * (1.0 + scale[None]) + shift[None]
    return shaped.reshape(values.shape)

def blocked(inputs, weight, blocks, mixer):
    rows, depth = inputs.shape
    span = depth // blocks
    stacked_in = inputs.reshape(rows, blocks, span).transpose(1, 0, 2)
    stacked_w = weight.reshape(blocks, span, weight.shape[1])
    start_total = mixer(jnp.zeros((rows, weight.shape[1]), jnp.float32))

    def step(total, pair):
        term = mixer(jnp.dot(pair[0], pair[1], preferred_element_type=jnp.float32))
        term = lax.optimization_barrier(term.astype(jnp.bfloat16)).astype(jnp.float32)
        return (total + term, None)
    result, unused = lax.scan(step, start_total, (stacked_in, stacked_w))
    return result

def keep_rows(values):
    return values

def attend(triple):
    query, keys, values = triple
    scores = jnp.einsum('qhd,khd->hqk', query.astype(jnp.float32), keys.astype(jnp.float32)) / jnp.sqrt(jnp.float32(HEAD_DIM))
    top = lax.optimization_barrier(jnp.max(scores, axis=-1, keepdims=True))
    weights = jnp.exp(scores - top)
    denom = lax.optimization_barrier(jnp.sum(weights, axis=-1))
    rounded = lax.optimization_barrier(weights.astype(jnp.bfloat16)).astype(jnp.float32)
    mixed = jnp.einsum('hqk,khd->qhd', rounded, values.astype(jnp.float32))
    return mixed / jnp.transpose(denom)[:, :, None]

def reference(clip_tokens, modulation, w_qkv, w_out, w_up, up_bias, w_down, guide_num):
    x_rows = clip_tokens.astype(jnp.float32)
    first = normalize(x_rows, modulation[:, 0], modulation[:, 1]).astype(jnp.bfloat16)
    qkv = blocked(first, w_qkv.reshape(D, 3 * INNER), N_ROW, keep_rows).astype(jnp.bfloat16)

    def split_heads(block):
        return block.reshape(SEQ, BRANCHES, HEADS, HEAD_DIM).transpose(1, 0, 2, 3)
    query = split_heads(qkv[:, :INNER])
    keys = split_heads(qkv[:, INNER:2 * INNER])
    values = split_heads(qkv[:, 2 * INNER:])
    mixed = lax.map(attend, (query, keys, values))
    att = mixed.transpose(1, 0, 2, 3).reshape(TOKENS, INNER).astype(jnp.bfloat16)
    out_rows = blocked(att, w_out, N_COL, keep_rows)
    gate_one = jnp.tile(modulation[:, 2], (SEQ, 1))
    resid = x_rows + gate_one * out_rows
    second = normalize(resid, modulation[:, 3], modulation[:, 4]).astype(jnp.bfloat16)
    up_rows = blocked(second, w_up, N_ROW, keep_rows)
    act = jax.nn.gelu(up_rows + up_bias[None], approximate=True).astype(jnp.bfloat16)
    guide_weights = guide_num.astype(jnp.float32) / 4.0
    weights_gate = guide_weights[:, None] * modulation[:, 5]

    def combine(partial_rows):
        return lax.optimization_barrier(jnp.sum(partial_rows.reshape(SEQ, BRANCHES, D) * weights_gate[None], axis=1))
    mlp_rows = blocked(act, w_down, N_COL, combine)
    resid_mix = lax.optimization_barrier(jnp.sum(resid.reshape(SEQ, BRANCHES, D) * guide_weights[None, :, None], axis=1))
    return (resid_mix + mlp_rows).astype(jnp.bfloat16)
```

```python
import functools

import jax
import jax.numpy as jnp
from jax import lax
from jax.experimental import pallas as pl
from jax.experimental.pallas import tpu as pltpu
from jax.sharding import PartitionSpec as P

HEAD_DIM = 128
BF = jnp.bfloat16
F32 = jnp.float32
eps = 1e-06
N = 4
GATHER_PARTS = ((2, 1, 1, 1), (2, 1, 1, 2))
REDUCE_PARTS = (2, 1, 1, 1)
MLP_PARTS = (1, 1, 1, 2)
ORDER = (
    "A0_0.0", "A0_0.1", "A1_0.0", "A1_0.1", "A2_0.0", "A2_0.1", "A0_1.0", "A3_0.0", "A3_0.1",
    "Q1_0", "Q2_0", "A1_1.0", "A2_1.0", "A3_1.0", "A0_2.0", "A0_3.0", "T1_0", "Q1_1",
    "Q2_1", "T2_0", "A1_2.0", "O_0", "A2_2.0", "T1_1", "A1_3.0", "A3_2.0", "Q1_2",
    "B1_0.0", "B1_0.1", "Q2_2", "T2_1", "A2_3.0", "B2_0.0", "O_1", "B2_0.1", "A3_3.0",
    "Q1_3", "N1_0", "B1_1.0", "T1_2", "N2_0", "Q2_3", "C0_0.1", "C0_0.0", "B2_1.0",
    "C1_0.1", "T2_2", "O_2", "C1_0.0", "T1_3", "C2_0.1", "B1_2.0", "N1_1", "C2_0.0",
    "T2_3", "N2_1", "C0_1.0", "O_3", "B2_2.0", "C3_0.0", "C3_0.1", "U1_0.0", "U2_0.0",
    "C1_1.0", "N1_2", "B1_3.0", "U3_0.0", "C2_1.0", "N2_2", "C0_2.0", "B2_3.0", "C3_1.0",
    "U1_1.0", "U2_1.0", "C1_2.0", "G_0.0", "N1_3", "U3_1.0", "C2_2.0", "W_0.0", "N2_3",
    "C3_2.0", "U1_2.0", "C0_3.1", "U2_2.0", "G_1.0", "C0_3.0", "U3_2.0", "C1_3.0", "W_1.0",
    "C2_3.0", "C3_3.0", "U1_3.0", "C1_3.1", "C2_3.1", "G_2.0", "U2_3.0", "U3_3.0", "C3_3.1",
    "W_2.0", "U1_3.1", "U2_3.1", "G_3.0", "U3_3.1", "W_3.0", "D0_0", "D1_0", "G_3.1",
    "W_3.1", "D0_1", "D1_1", "D2_0", "D2_1", "D3_0", "D3_1",
)


def normalize(values, shift, scale):
    totals = lax.psum((jnp.sum(values, axis=1), jnp.sum(values * values, axis=1)), "row")
    width = values.shape[1] * lax.axis_size("row")
    mean = totals[0] / width
    variance = totals[1] / width - mean * mean
    normed = (values - mean[:, None]) * lax.rsqrt(variance + eps)[:, None]
    branches = shift.shape[0]
    shaped = normed.reshape(-1, branches, values.shape[1]) * (1.0 + scale[None]) + shift[None]
    return shaped.reshape(values.shape)


def general_layer(clip_tokens, modulation, w_qkv, w_out, w_up, up_bias, w_down, guide_num):
    branches = modulation.shape[0]
    feat_rows = w_qkv.shape[0]
    head_cols = w_qkv.shape[2]
    heads_here = head_cols // HEAD_DIM
    x_rows = clip_tokens.astype(jnp.float32)
    first = normalize(x_rows, modulation[:, 0], modulation[:, 1]).astype(jnp.bfloat16)
    w_flat = w_qkv.reshape(feat_rows, 3 * head_cols)
    partial_qkv = jnp.dot(
        lax.all_gather(first, "col", axis=0, tiled=True), w_flat, preferred_element_type=jnp.float32
    )
    scale_score = 1.0 / jnp.sqrt(jnp.float32(HEAD_DIM))
    qkv = lax.psum_scatter(partial_qkv.astype(jnp.bfloat16), "row", scatter_dimension=0, tiled=True)
    query3 = qkv[:, :head_cols].reshape(-1, heads_here, HEAD_DIM)
    query_rows = query3.shape[0]
    piece = (
        lax.all_gather(qkv[:, head_cols : 2 * head_cols], "row", axis=0, tiled=True),
        lax.all_gather(qkv[:, 2 * head_cols :], "row", axis=0, tiled=True),
    )
    top = jnp.full((heads_here, query_rows), -1e30, jnp.float32)
    rows = piece[0].shape[0]
    key_heads = piece[0].reshape(rows, heads_here, HEAD_DIM)
    value_heads = piece[1].reshape(rows, heads_here, HEAD_DIM)
    scores = (
        jnp.einsum("qhd,khd->hqk", query3, key_heads, preferred_element_type=jnp.float32)
        * scale_score
    )
    query_branch = jnp.arange(query3.shape[0], dtype=jnp.int32) % branches
    key_branch = jnp.arange(rows, dtype=jnp.int32) % branches
    allowed = (query_branch[:, None] == key_branch[None, :])[None]
    masked = jnp.where(allowed, scores, -1e30)
    new_top = jnp.maximum(top, jnp.max(masked, axis=-1))
    weights = jnp.where(allowed, jnp.exp(masked - new_top[..., None]), 0.0)
    denom = jnp.sum(weights, axis=-1)
    accum = jnp.einsum(
        "hqk,khd->hqd",
        weights.astype(jnp.bfloat16),
        value_heads,
        preferred_element_type=jnp.float32,
    )
    att = (accum / denom[..., None]).transpose(1, 0, 2).reshape(-1, head_cols).astype(jnp.bfloat16)
    partial_out = jnp.dot(
        lax.all_gather(att, "row", axis=0, tiled=True), w_out, preferred_element_type=jnp.float32
    )
    out_rows = lax.psum_scatter(
        partial_out.astype(jnp.bfloat16), "col", scatter_dimension=0, tiled=True
    ).astype(jnp.float32)
    by_branch = x_rows.shape[0] // branches
    resid = (
        x_rows.reshape(by_branch, branches, feat_rows)
        + modulation[None, :, 2] * out_rows.reshape(by_branch, branches, feat_rows)
    ).reshape(x_rows.shape)
    second = normalize(resid, modulation[:, 3], modulation[:, 4]).astype(jnp.bfloat16)
    partial_up = jnp.dot(
        lax.all_gather(second, "col", axis=0, tiled=True), w_up, preferred_element_type=jnp.float32
    )
    up_rows = lax.psum_scatter(
        partial_up.astype(jnp.bfloat16), "row", scatter_dimension=0, tiled=True
    ).astype(jnp.float32)
    act = jax.nn.gelu(up_rows + up_bias[None], approximate=True).astype(jnp.bfloat16)
    partial_down = jnp.dot(
        lax.all_gather(act, "row", axis=0, tiled=True), w_down, preferred_element_type=jnp.float32
    )
    guide_weights = guide_num.astype(jnp.float32) / 4.0
    weights_gate = guide_weights[:, None] * modulation[:, 5]
    combined = jnp.sum(partial_down.reshape(-1, branches, feat_rows) * weights_gate[None], axis=1)
    mlp_rows = lax.psum_scatter(
        combined.astype(jnp.bfloat16), "col", scatter_dimension=0, tiled=True
    ).astype(jnp.float32)
    resid_mix = jnp.sum(
        resid.reshape(by_branch, branches, feat_rows) * guide_weights[None, :, None], axis=1
    )
    return (resid_mix + mlp_rows).astype(jnp.bfloat16)


class Move:
    def __init__(self, src, dst, send, recv, to, sent=None, got=None):
        self.copy = pltpu.make_async_remote_copy(
            src_ref=src, dst_ref=dst, send_sem=send, recv_sem=recv, device_id=to,
            device_id_type=pl.DeviceIdType.MESH,
        )
        self.sent = sent

    def start(self):
        run(self.sent, self.copy.start)

    def wait_send(self):
        run(self.sent, self.copy.wait_send)


def run(cond, act):
    if cond is None:
        act()
    else:
        pl.when(cond)(lambda: act() and None)


def received(dst, recv, send, to):
    pltpu.make_async_remote_copy(
        src_ref=dst, dst_ref=dst, send_sem=send, recv_sem=recv, device_id=to,
        device_id_type=pl.DeviceIdType.MESH,
    ).wait_recv()


def layer_kernel(
    x_hbm, mod, wq_hbm, wo_hbm, wu_hbm, bias, wd_hbm, guide, out,
    xa, wq, wu, wo, wd, sb, ownq, ownu, r1, r2, att, acto, pb, rb, res, acc, xs, st, mom1, mom2,
    lx, lq, lu, lo, ld, s_mom1, r_mom1, s_mom2, r_mom2, s_gat, r_gat, s_red, r_red, s_core, r_core,
    s_x, r_x, s_att, r_att,
):
    r, z = lax.axis_index("row"), lax.axis_index("col")
    core = lax.rem(r, 2)
    chunk, width = xa.shape[2], xa.shape[3]
    tokens = N * chunk
    bw = wq.shape[2]
    half = 6 * bw
    feats = 4 * width
    tile = 256 if width % 256 == 0 else 128
    mate, across, diag = {"row": r ^ 1}, {"row": r ^ 2}, {"row": r ^ 3}
    above, below = {"col": jnp.minimum(z + 1, N - 1)}, {"col": jnp.maximum(z - 1, 0)}

    local_x = pltpu.make_async_copy(x_hbm, sb.at[0, :, 0:width], lx)
    local_x.start()
    loads = {"q": [], "o": [], "u": [], "d": []}
    for i in (6, 7, 8, 9, 10, 11, 0, 1, 2, 3, 4, 5):
        owner = r ^ (0, 2, 1, 3)[i // 3]
        cols = pl.ds(pl.multiple_of(owner * bw, bw), bw)
        loads["q"].append(pltpu.make_async_copy(wq_hbm.at[i % 3, :, cols], wq.at[i], lq.at[i]))
    for i in range(4):
        owner = r ^ (0, 2, 1, 3)[i]
        rows = pl.ds(pl.multiple_of(owner * bw, bw), bw)
        loads["o"].append(pltpu.make_async_copy(wo_hbm.at[rows], wo.at[pl.ds(i * bw, bw)], lo.at[i]))
    for i in (6, 7, 8, 9, 10, 11, 0, 1, 2, 3, 4, 5):
        side = core if i < 6 else 1 - core
        cols = pl.ds(pl.multiple_of(side * half + (i % 6) * bw, bw), bw)
        loads["u"].append(pltpu.make_async_copy(wu_hbm.at[:, cols], wu.at[i], lu.at[i]))
    for i in range(2):
        side = core if i == 0 else 1 - core
        rows = pl.ds(pl.multiple_of(side * half, bw), half)
        loads["d"].append(pltpu.make_async_copy(wd_hbm.at[rows], wd.at[i], ld.at[i]))

    def ready(name, only=None):
        for i, load in enumerate(loads[name]):
            if only is None or i in only:
                load.wait()

    barrier = pltpu.get_barrier_semaphore()

    def greet(to, cond=None):
        run(cond, lambda: pl.semaphore_signal(barrier, inc=1, device_id=to, device_id_type=pl.DeviceIdType.MESH))

    for to in (mate, across, diag):
        greet(to)
    greet(above, z < N - 1)
    greet(below, z > 0)
    inner = (z > 0) & (z < N - 1)
    run(inner, lambda: pl.semaphore_wait(barrier, 5))
    run(jnp.logical_not(inner), lambda: pl.semaphore_wait(barrier, 4))

    local_x.wait()
    for group in loads.values():
        for load in group:
            load.start()

    pending = {}

    def send(key, moves):
        pending[key] = moves
        for move in moves:
            move.start()

    def settle(key):
        for move in pending.pop(key, []):
            move.wait_send()

    def stats_rows(values, into, rows):
        total = jnp.sum(values, axis=1, keepdims=True)
        squares = jnp.sum(values * values, axis=1, keepdims=True)
        lane = lax.broadcasted_iota(jnp.int32, (values.shape[0], 128), 1)
        into[rows, :] = jnp.where(lane == 0, total, squares)

    def scales(total):
        mean = total[0:1] / feats
        rstd = lax.rsqrt(total[1:2] / feats - mean * mean + eps)
        lane = lax.broadcasted_iota(jnp.int32, (128, total.shape[1]), 0)
        return jnp.where(lane == 0, mean, rstd).T

    for i in range(width // 128):
        cols = slice(i * 128, (i + 1) * 128)
        xs[i % 2] = sb[0, :, cols].astype(F32)
        for b in range(N):
            res[b, :, cols] = xs[i % 2, pl.ds(b, chunk, stride=N), :]
    for b in range(N):
        stats_rows(res[b], st, slice(b * chunk, (b + 1) * chunk))
    mom1[0] = st[...].T[0:8]
    send("mom1", [
        Move(mom1.at[0], mom1.at[m], s_mom1.at[m - 1], r_mom1.at[m - 1], to)
        for m, to in ((1, mate), (2, across), (3, diag))
    ])
    for m in (1, 2, 3):
        received(mom1.at[m], r_mom1.at[m - 1], s_mom1.at[m - 1], mate)
    st[...] = scales(mom1[0] + mom1[1] + mom1[2] + mom1[3])

    def part_rows(parts, p):
        return slice(p * (chunk // parts), (p + 1) * (chunk // parts))

    def gather_start(stage, b, p):
        mine = xa.at[b, z, part_rows(GATHER_PARTS[stage][b], p)]
        sends, gets = s_gat.at[stage, b, p], r_gat.at[stage, b, p]
        up = Move(mine, mine, sends.at[0, 0], gets.at[0, 0], above, z < N - 1)
        down = Move(mine, mine, sends.at[1, 0], gets.at[1, 0], below, z > 0)
        send(("gat", stage, b, p, 0), [up, down])

    def gather_hop(stage, b, p, h):
        low, high = jnp.maximum(z - h, 0), jnp.minimum(z + h, N - 1)
        rows = part_rows(GATHER_PARTS[stage][b], p)
        sends, gets = s_gat.at[stage, b, p], r_gat.at[stage, b, p]
        moves = []

        def hop(side, at, here, on, to):
            data = xa.at[b, at, rows]
            run(here, lambda: received(data, gets.at[side, h - 1], sends.at[side, 0], to))
            if h < N - 1:
                move = Move(data, data, sends.at[side, h], gets.at[side, h], to, here & on)
                move.start()
                moves.append(move)

        hop(0, low, z >= h, z < N - 1, above)
        hop(1, high, z + h <= N - 1, z > 0, below)
        pending[("gat", stage, b, p, h)] = moves

    def settle_gather(stage, b):
        for p in range(GATHER_PARTS[stage][b]):
            for h in range(N):
                settle(("gat", stage, b, p, h))

    def red_move(b, key, slot, rows, p, side, j):
        k = j if side == 0 else N - 1 - j
        to = below if side == 0 else above
        return pb.at[slot, k, rows], rb.at[key, side, j, rows], s_red.at[b, p, side, j], r_red.at[b, p, side, j], to

    def reduce_start(b, key, slot, rows, p):
        moves = []
        for j in range(N - 1):
            moves.append(Move(*red_move(b, key, slot, rows, p, 0, j), z == N - 1))
            moves.append(Move(*red_move(b, key, slot, rows, p, 1, j), z == 0))
        send(("red", b, p, 0), moves)

    def reduce_hop(b, key, slot, rows, p, t):
        moves = []

        def hop(side, j, valid):
            j = jnp.clip(j, 0, N - 2)
            src, dst, ss, rs, to = red_move(b, key, slot, rows, p, side, j)

            @pl.when(valid)
            def _():
                received(dst, rs, ss, to)
                k = j if side == 0 else N - 1 - j
                pb[slot, k, rows] = (pb[slot, k, rows].astype(F32) + rb[key, side, j, rows].astype(F32)).astype(BF)

            move = Move(src, dst, ss, rs, to, valid)
            move.start()
            moves.append(move)

        down, up = t - (N - 1 - z), t - z
        hop(0, down, (z < N - 1) & (down >= 0) & (down < z))
        hop(1, up, (z > 0) & (up >= 0) & (up < N - 1 - z))
        pending[("red", b, p, t)] = moves

    def reduce_end(b, key, rows, p, add):
        for side, j, valid in ((0, z, z < N - 1), (1, N - 1 - z, z > 0)):
            j = jnp.minimum(j, N - 2)

            def take(side=side, j=j):
                received(rb.at[key, side, j, rows], r_red.at[b, p, side, j], s_red.at[b, p, side, j], mate)
                add(rb[key, side, j, rows].astype(F32))

            run(valid, take)

    def settle_reduce(b):
        for p in range(2):
            for t in range(N - 1):
                settle(("red", b, p, t))

    order = list(ORDER)
    for b in range(N):
        sc = st[b * chunk : (b + 1) * chunk, :]
        normed = (res[b] - sc[:, 0:1]) * sc[:, 1:2]
        xa[b, z] = (normed * (1.0 + mod[1, b : b + 1, :]) + mod[0, b : b + 1, :]).astype(BF)
        while order and order[0].split("_")[0] == "A0" and int(order[0][3]) == b:
            gather_start(0, b, int(order.pop(0)[5]))

    def project(b, rows, weight, first, target):
        def body(i, carry):
            cols = pl.ds(pl.multiple_of(i * bw, bw), bw)
            left = xa[b, :, rows].reshape(-1, width)
            target[:, cols] = jnp.dot(left, weight[first + i], preferred_element_type=F32).astype(BF)
            return carry

        lax.fori_loop(0, 6, body, 0)

    def project_all(stage, b, rows, span, s, weight, own, name):
        settle(("core", s))
        if b == 0 and name:
            ready(name, range(6))
        project(b, rows, weight, 6, sb.at[s, span])
        send(("core", s), [Move(sb.at[s, span], r1.at[b, span], s_core.at[stage, b], r_core.at[stage, b], mate)])
        if b == 0 and name:
            ready(name, range(6, 12))
        settle(("own", stage > 0, s))
        project(b, rows, weight, 0, own.at[s, span])

    def pair_sum(own, s, b, span, cols):
        own[s, span, cols] = (own[s, span, cols].astype(F32) + r1[b, span, cols].astype(F32)).astype(BF)

    def do_A(h, b, p):
        if h == 0:
            gather_start(0, b, p)
        else:
            gather_hop(0, b, p, h)

    whole, all_rows = slice(0, tokens), slice(0, chunk)

    def do_Q1(b):
        project_all(0, b, all_rows, whole, b % 2, wq, ownq, "q")

    def do_Q2(b):
        received(r1.at[b], r_core.at[0, b], s_core.at[0, b], mate)
        for i in range(3, 6):
            pair_sum(ownq, b % 2, b, whole, slice(i * bw, (i + 1) * bw))
        send(("own", False, b % 2), [
            Move(ownq.at[b % 2, :, 3 * bw : half], r2.at[b, :, 0 : 3 * bw], s_x.at[0, b], r_x.at[0, b], across)])

    def do_T1(b):
        received(r2.at[b, :, 0 : 3 * bw], r_x.at[0, b], s_x.at[0, b], across)
        qkv = []
        for j in range(3):
            cols = slice(j * bw, (j + 1) * bw)
            total = ownq[b % 2, :, cols].astype(F32) + r1[b, :, cols].astype(F32) + r2[b, :, cols].astype(F32)
            qkv.append(total.astype(BF))
        for h in range(bw // HEAD_DIM):
            cols = slice(h * HEAD_DIM, (h + 1) * HEAD_DIM)
            scores = lax.dot_general(
                qkv[0][:, cols], qkv[1][:, cols], (((1,), (1,)), ((), ())), preferred_element_type=F32)
            scores = scores * (1.0 / HEAD_DIM**0.5)
            weights = jnp.exp(scores - jnp.max(scores, axis=-1, keepdims=True))
            denom = jnp.sum(weights, axis=-1, keepdims=True)
            mixed = jnp.dot(weights.astype(BF), qkv[2][:, cols], preferred_element_type=F32)
            att[b, :, cols] = (mixed / denom).astype(BF)
        send(("att", b, 0), [
            Move(att.at[b, :, 0:bw], att.at[b, :, bw : 2 * bw], s_att.at[b, 0], r_att.at[b, 0], across),
            Move(att.at[b, :, 0:bw], att.at[b, :, 2 * bw : 3 * bw], s_att.at[b, 1], r_att.at[b, 1], mate),
        ])

    def do_T2(b):
        received(att.at[b, :, bw : 2 * bw], r_att.at[b, 0], s_att.at[b, 0], across)
        send(("att", b, 1), [
            Move(att.at[b, :, bw : 2 * bw], att.at[b, :, 3 * bw : 4 * bw], s_att.at[b, 2], r_att.at[b, 2], mate)])

    def do_O(b):
        received(att.at[b, :, 2 * bw : 3 * bw], r_att.at[b, 1], s_att.at[b, 1], mate)
        received(att.at[b, :, 3 * bw : 4 * bw], r_att.at[b, 2], s_att.at[b, 2], mate)
        if b == 0:
            ready("o")
        if b >= 2:
            settle_reduce(b - 2)
        settle_gather(0, b)

        def body(i, carry):
            cols = pl.ds(pl.multiple_of(i * tile, tile), tile)
            part = jnp.dot(att[b], wo[:, cols], preferred_element_type=F32).astype(BF)
            pb[b % 2, :, :, cols] = part.reshape(N, chunk, tile)
            return carry

        lax.fori_loop(0, width // tile, body, 0)
        for p in range(REDUCE_PARTS[b]):
            reduce_start(b, b, b % 2, part_rows(REDUCE_PARTS[b], p), p)

    def do_B(t, b, p):
        reduce_hop(b, b, b % 2, part_rows(REDUCE_PARTS[b], p), p, t)

    def do_N1(b):
        gate = mod[2, b : b + 1, :]
        res[b] = res[b] + gate * pb[b % 2, z].astype(F32)

        for p in range(REDUCE_PARTS[b]):
            rows = part_rows(REDUCE_PARTS[b], p)

            def add(part, rows=rows):
                res[b, rows] = res[b, rows] + gate * part

            reduce_end(b, b, rows, p, add)
        stats_rows(res[b], st, slice(0, chunk))
        mom2[b, 0] = st[0:128, :].T[0:8]
        send(("mom2", b), [
            Move(mom2.at[b, 0], mom2.at[b, m], s_mom2.at[b, m - 1], r_mom2.at[b, m - 1], to)
            for m, to in ((1, mate), (2, across), (3, diag))
        ])

    def do_N2(b):
        for m in (1, 2, 3):
            received(mom2.at[b, m], r_mom2.at[b, m - 1], s_mom2.at[b, m - 1], mate)
        sc = scales(mom2[b, 0] + mom2[b, 1] + mom2[b, 2] + mom2[b, 3])[0:chunk]
        normed = (res[b] - sc[:, 0:1]) * sc[:, 1:2]
        xa[b, z] = (normed * (1.0 + mod[4, b : b + 1, :]) + mod[3, b : b + 1, :]).astype(BF)

    def do_C(h, b, p):
        if h == 0:
            gather_start(1, b, p)
        else:
            gather_hop(1, b, p, h)

    units = [(b, q) for b in range(N) for q in range(MLP_PARTS[b])]

    def unit(b, q):
        parts = MLP_PARTS[b]
        count = tokens // parts
        return units.index((b, q)) % 2, part_rows(parts, q), slice(q * count, (q + 1) * count)

    def do_U1(b, q):
        s, rows, span = unit(b, q)
        project_all(1 + q, b, rows, span, s, wu, ownu, "u" if q == 0 else "")

    def up_move(b, q, part):
        s, _, span = unit(b, q)
        cols = slice(part * 3 * bw, (part + 1) * 3 * bw)
        sem = 1 + 2 * q + part
        return Move(ownu.at[s, span, cols], r2.at[b, span, cols], s_x.at[sem, b], r_x.at[sem, b], across)

    def do_U(b, q, part):
        s, _, span = unit(b, q)
        if part == 0:
            received(r1.at[b, span], r_core.at[1 + q, b], s_core.at[1 + q, b], mate)
        for i in range(3 * part, 3 * part + 3):
            pair_sum(ownu, s, b, span, slice(i * bw, (i + 1) * bw))
        send(("ux", b, q, part), [up_move(b, q, part)])

    def do_G(b, q):
        s, _, span = unit(b, q)
        for part in range(2):
            settle(("ux", b, q, part))
            up_move(b, q, part).copy.wait_recv()

        def body(i, carry):
            cols = pl.ds(pl.multiple_of(i * bw, bw), bw)
            up = ownu[s, span, cols].astype(F32) + r2[b, span, cols].astype(F32)
            up = up + bias[:, pl.ds(pl.multiple_of(core * half + i * bw, bw), bw)]
            ownu[s, span, cols] = jax.nn.gelu(up, approximate=True).astype(BF)
            return carry

        lax.fori_loop(0, 6, body, 0)
        send(("own", True, s), [
            Move(ownu.at[s, span], acto.at[b, span], s_core.at[3 + q, b], r_core.at[3 + q, b], mate)])

    def do_W(b, q):
        s, rows, span = unit(b, q)
        received(acto.at[b, span], r_core.at[3 + q, b], s_core.at[3 + q, b], mate)
        if (b, q) == (0, 0):
            ready("d")
        scale = guide[b].astype(F32) * 0.25

        def body(i, carry):
            cols = pl.ds(pl.multiple_of(i * tile, tile), tile)
            down = jnp.dot(ownu[s, span], wd[0, :, cols], preferred_element_type=F32)
            down = down + jnp.dot(acto[b, span], wd[1, :, cols], preferred_element_type=F32)
            down = (down * (mod[5, b : b + 1, cols] * scale)).reshape(N, -1, tile)
            acc[:, rows, cols] = down if b == 0 else acc[:, rows, cols] + down
            return carry

        lax.fori_loop(0, width // tile, body, 0)

    def do_D(t, q):
        rows = part_rows(MLP_PARTS[N - 1], q)
        if t == 0:
            settle_reduce(2)
            pb[0, :, rows] = acc[:, rows].astype(BF)
            reduce_start(N, 0, 0, rows, q)
        elif t < N - 1:
            reduce_hop(N, 0, 0, rows, q, t)
        else:
            total = acc[z, rows]
            for b in range(N):
                total = total + (guide[b].astype(F32) * 0.25) * res[b, rows]
            acc[z, rows] = total

            def finish(part):
                acc[z, rows] = acc[z, rows] + part

            reduce_end(N, 0, rows, q, finish)
            out[rows] = acc[z, rows].astype(BF)

    for event in order:
        name, where = event.split("_")
        args = [int(v) for v in where.split(".")]
        if name[0] in "ABCD":
            {"A": do_A, "B": do_B, "C": do_C, "D": do_D}[name[0]](int(name[1]), *args)
        elif name in ("U2", "U3"):
            do_U(*args, int(name[1]) - 2)
        else:
            {"Q1": do_Q1, "Q2": do_Q2, "T1": do_T1, "T2": do_T2, "O": do_O, "N1": do_N1, "N2": do_N2,
             "U1": do_U1, "G": do_G, "W": do_W}[name](*args)
    for key in list(pending):
        settle(key)


def fused_layer(clip_tokens, modulation, w_qkv, w_out, w_up, up_bias, w_down, guide_num):
    rows, width = clip_tokens.shape
    chunk = rows // N
    heads = w_qkv.shape[2]
    bw = heads // 4
    half = 6 * bw
    dma, vmem, anywhere = pltpu.SemaphoreType.DMA, pltpu.VMEM, pl.BlockSpec(memory_space=pl.ANY)
    inside = pl.BlockSpec(memory_space=pltpu.VMEM)
    scratch = [
        vmem((N, N, chunk, width), BF),
        vmem((12, width, bw), BF),
        vmem((12, width, bw), BF),
        vmem((heads, width), BF),
        vmem((2, half, width), BF),
        vmem((2, rows, half), BF),
        vmem((2, rows, half), BF),
        vmem((2, rows, half), BF),
        vmem((N, rows, half), BF),
        vmem((N, rows, half), BF),
        vmem((N, rows, heads), BF),
        vmem((N, rows, half), BF),
        vmem((2, N, chunk, width), BF),
        vmem((N, 2, N - 1, chunk, width), BF),
        vmem((N, chunk, width), F32),
        vmem((N, chunk, width), F32),
        vmem((2, rows, 128), F32),
        vmem((max(rows, 128), 128), F32),
        vmem((N, 8, max(rows, 128)), F32),
        vmem((N, N, 8, 128), F32),
        dma, dma((12,)), dma((12,)), dma((4,)), dma((2,)),
        dma((3,)), dma((3,)), dma((N, 3)), dma((N, 3)),
        dma((2, N, 2, 2, N - 1)), dma((2, N, 2, 2, N - 1)),
        dma((N + 1, 2, 2, N - 1)), dma((N + 1, 2, 2, N - 1)),
        dma((5, N)), dma((5, N)), dma((5, N)), dma((5, N)), dma((N, 3)), dma((N, 3)),
    ]
    return pl.pallas_call(
        layer_kernel,
        out_shape=jax.ShapeDtypeStruct((chunk, width), BF),
        in_specs=[anywhere, inside, anywhere, anywhere, anywhere, inside, anywhere,
                  pl.BlockSpec(memory_space=pltpu.SMEM)],
        out_specs=inside,
        scratch_shapes=scratch,
        compiler_params=pltpu.CompilerParams(
            collective_id=0, has_side_effects=True, vmem_limit_bytes=121 * 512 * 1024),
    )(
        clip_tokens, modulation.transpose(1, 0, 2), w_qkv.transpose(1, 0, 2), w_out, w_up,
        up_bias[None], w_down, guide_num,
    )


def on_device(*args):
    tokens, modulation, w_qkv, _, w_up = args[:5]
    head_cols = w_qkv.shape[2]
    square = lax.axis_size("row") == 4 and lax.axis_size("col") == 4 and modulation.shape[0] == 4
    if square and head_cols % 512 == 0 and w_up.shape[1] == 3 * head_cols and tokens.shape[0] % 128 == 0:
        return fused_layer(*args)
    return general_layer(*args)


def solution(mesh):
    in_specs = (
        P(("clips", "col"), "row"),
        P("clips", None, "row"),
        P("row", None, "col"),
        P("col", "row"),
        P("row", "col"),
        P("col"),
        P("col", "row"),
        P("clips"),
    )
    out_specs = P(("clips", "col"), "row")
    return jax.shard_map(
        on_device, mesh=mesh, in_specs=in_specs, out_specs=out_specs, check_vma=False
    )
```

```python
import functools

import jax
import jax.numpy as jnp
from jax import lax
from jax.experimental import pallas as pl
from jax.experimental.pallas import tpu as pltpu
from jax.sharding import PartitionSpec as P

HEAD_DIM = 128
BF = jnp.bfloat16
F32 = jnp.float32
eps = 1e-06
N = 4
IN_PARTS = ((2, 2), (1, 3), (2, 2), (1, 1, 2))
Q_SPLIT = (1, 1, 1, 1)
PARTS = ((2, 2), (2, 2), (2, 1, 1), (2, 1, 1))
MOST = 3
ORDER = (
    "A0_0.0", "A0_0.1", "A1_0.0", "A1_0.1", "A2_0.0", "A0_1.0", "A2_0.1", "A3_0.0", "A0_1.1",
    "Q1_0.0", "Q2_0.0", "A1_1.0", "A3_0.1", "Q1_0.1", "Q2_0.1", "A2_1.0", "A3_1.0", "A1_1.1",
    "Q1_1.0", "A2_1.1", "A0_2.0", "A0_2.1", "Q2_1.0", "A0_3.0", "T1_0", "A3_1.1", "Q1_1.1",
    "A0_3.1", "Q2_1.1", "A0_3.2", "A1_2.0", "T2_0", "O_0", "A2_2.0", "A1_2.1", "T1_1",
    "A3_2.0", "A1_3.1", "A1_3.0", "Q1_2.0", "A2_2.1", "A1_3.2", "T2_1", "Q2_2.0", "B1_0.0",
    "O_1", "B1_0.1", "A2_3.1", "A3_2.1", "Q1_2.1", "A2_3.0", "Q2_2.1", "A3_3.1", "B2_0.0",
    "A3_3.0", "Q1_3.0", "A2_3.2", "B2_0.1", "Q1_3.1", "N1_0.0", "Q2_3.1", "B1_1.0", "T1_2",
    "N2_0.0", "C0_0.0", "B2_1.0", "N1_0.1", "A3_3.2", "Q2_3.0", "B1_1.1", "Q1_3.2", "T2_2",
    "N2_0.1", "Q2_3.2", "C0_0.1", "C1_0.0", "N1_1.0", "B2_1.1", "O_2", "N2_1.0", "C2_0.0",
    "T1_3", "C1_0.1", "B1_2.0", "N1_1.1", "C3_0.0", "U1_0.0", "U2_0.0", "T2_3", "C2_0.1",
    "C0_1.0", "U3_0.0", "N2_1.1", "B2_2.0", "C0_1.1", "O_3", "C3_0.1", "U1_0.1", "U2_0.1",
    "B1_2.1", "C1_1.0", "U3_0.1", "B2_2.1", "G_0.0", "B1_2.2", "N1_2.0", "C2_1.0", "B1_3.0",
    "W_0.0", "N1_2.1", "C3_1.0", "C1_1.1", "U1_1.0", "B2_3.0", "U2_1.0", "B2_2.2", "G_0.1",
    "C2_1.1", "N2_2.0", "C0_2.0", "N2_2.1", "C0_2.1", "U3_1.0", "W_0.1", "C3_1.1", "B1_3.2",
    "U1_1.1", "N1_3.0", "C1_2.0", "N1_2.2", "B2_3.2", "U2_1.1", "G_1.0", "U3_1.1", "C2_2.0",
    "N2_3.0", "C0_3.0", "B1_3.1", "W_1.0", "C3_2.0", "C1_2.1", "N2_2.2", "U1_2.0", "U2_2.0",
    "U3_2.0", "C0_2.2", "N1_3.2", "C2_2.1", "B2_3.1", "C1_2.2", "G_1.1", "C3_2.1", "C1_3.0",
    "W_1.1", "C2_2.2", "N1_3.1", "U1_2.1", "U2_2.1", "G_2.0", "C2_3.0", "U3_2.1", "N2_3.1",
    "C0_3.1", "C3_2.2", "W_2.0", "U1_2.2", "C3_3.0", "G_2.1", "U2_2.2", "U3_2.2", "N2_3.2",
    "C1_3.1", "W_2.1", "U1_3.0", "C0_3.2", "C2_3.1", "U2_3.0", "U3_3.0", "C1_3.2", "C2_3.2",
    "G_2.2", "W_2.2", "C3_3.1", "U1_3.1", "G_3.0", "U2_3.1", "U3_3.1", "C3_3.2", "W_3.0",
    "U1_3.2", "D0_0", "U2_3.2", "U3_3.2", "D1_0", "G_3.1", "W_3.1", "D0_1", "G_3.2",
    "D2_0", "W_3.2", "D0_2", "D1_1", "D1_2", "D2_1", "D2_2", "D3_1", "D3_0",
    "D3_2",
)


def normalize(values, shift, scale):
    totals = lax.psum((jnp.sum(values, axis=1), jnp.sum(values * values, axis=1)), "row")
    width = values.shape[1] * lax.axis_size("row")
    mean = totals[0] / width
    variance = totals[1] / width - mean * mean
    normed = (values - mean[:, None]) * lax.rsqrt(variance + eps)[:, None]
    branches = shift.shape[0]
    shaped = normed.reshape(-1, branches, values.shape[1]) * (1.0 + scale[None]) + shift[None]
    return shaped.reshape(values.shape)


def general_layer(clip_tokens, modulation, w_qkv, w_out, w_up, up_bias, w_down, guide_num):
    branches = modulation.shape[0]
    feat_rows = w_qkv.shape[0]
    head_cols = w_qkv.shape[2]
    heads_here = head_cols // HEAD_DIM
    x_rows = clip_tokens.astype(jnp.float32)
    first = normalize(x_rows, modulation[:, 0], modulation[:, 1]).astype(jnp.bfloat16)
    w_flat = w_qkv.reshape(feat_rows, 3 * head_cols)
    partial_qkv = jnp.dot(
        lax.all_gather(first, "col", axis=0, tiled=True), w_flat, preferred_element_type=jnp.float32
    )
    scale_score = 1.0 / jnp.sqrt(jnp.float32(HEAD_DIM))
    qkv = lax.psum_scatter(partial_qkv.astype(jnp.bfloat16), "row", scatter_dimension=0, tiled=True)
    query3 = qkv[:, :head_cols].reshape(-1, heads_here, HEAD_DIM)
    query_rows = query3.shape[0]
    piece = (
        lax.all_gather(qkv[:, head_cols : 2 * head_cols], "row", axis=0, tiled=True),
        lax.all_gather(qkv[:, 2 * head_cols :], "row", axis=0, tiled=True),
    )
    top = jnp.full((heads_here, query_rows), -1e30, jnp.float32)
    rows = piece[0].shape[0]
    key_heads = piece[0].reshape(rows, heads_here, HEAD_DIM)
    value_heads = piece[1].reshape(rows, heads_here, HEAD_DIM)
    scores = (
        jnp.einsum("qhd,khd->hqk", query3, key_heads, preferred_element_type=jnp.float32)
        * scale_score
    )
    query_branch = jnp.arange(query3.shape[0], dtype=jnp.int32) % branches
    key_branch = jnp.arange(rows, dtype=jnp.int32) % branches
    allowed = (query_branch[:, None] == key_branch[None, :])[None]
    masked = jnp.where(allowed, scores, -1e30)
    new_top = jnp.maximum(top, jnp.max(masked, axis=-1))
    weights = jnp.where(allowed, jnp.exp(masked - new_top[..., None]), 0.0)
    denom = jnp.sum(weights, axis=-1)
    accum = jnp.einsum(
        "hqk,khd->hqd",
        weights.astype(jnp.bfloat16),
        value_heads,
        preferred_element_type=jnp.float32,
    )
    att = (accum / denom[..., None]).transpose(1, 0, 2).reshape(-1, head_cols).astype(jnp.bfloat16)
    partial_out = jnp.dot(
        lax.all_gather(att, "row", axis=0, tiled=True), w_out, preferred_element_type=jnp.float32
    )
    out_rows = lax.psum_scatter(
        partial_out.astype(jnp.bfloat16), "col", scatter_dimension=0, tiled=True
    ).astype(jnp.float32)
    by_branch = x_rows.shape[0] // branches
    resid = (
        x_rows.reshape(by_branch, branches, feat_rows)
        + modulation[None, :, 2] * out_rows.reshape(by_branch, branches, feat_rows)
    ).reshape(x_rows.shape)
    second = normalize(resid, modulation[:, 3], modulation[:, 4]).astype(jnp.bfloat16)
    partial_up = jnp.dot(
        lax.all_gather(second, "col", axis=0, tiled=True), w_up, preferred_element_type=jnp.float32
    )
    up_rows = lax.psum_scatter(
        partial_up.astype(jnp.bfloat16), "row", scatter_dimension=0, tiled=True
    ).astype(jnp.float32)
    act = jax.nn.gelu(up_rows + up_bias[None], approximate=True).astype(jnp.bfloat16)
    partial_down = jnp.dot(
        lax.all_gather(act, "row", axis=0, tiled=True), w_down, preferred_element_type=jnp.float32
    )
    guide_weights = guide_num.astype(jnp.float32) / 4.0
    weights_gate = guide_weights[:, None] * modulation[:, 5]
    combined = jnp.sum(partial_down.reshape(-1, branches, feat_rows) * weights_gate[None], axis=1)
    mlp_rows = lax.psum_scatter(
        combined.astype(jnp.bfloat16), "col", scatter_dimension=0, tiled=True
    ).astype(jnp.float32)
    resid_mix = jnp.sum(
        resid.reshape(by_branch, branches, feat_rows) * guide_weights[None, :, None], axis=1
    )
    return (resid_mix + mlp_rows).astype(jnp.bfloat16)


class Move:
    def __init__(self, src, dst, send, recv, to, sent=None, got=None):
        self.copy = pltpu.make_async_remote_copy(
            src_ref=src, dst_ref=dst, send_sem=send, recv_sem=recv, device_id=to,
            device_id_type=pl.DeviceIdType.MESH,
        )
        self.sent = sent

    def start(self):
        run(self.sent, self.copy.start)

    def wait_send(self):
        run(self.sent, self.copy.wait_send)


def run(cond, act):
    if cond is None:
        act()
    else:
        pl.when(cond)(lambda: act() and None)


def received(dst, recv, send, to):
    pltpu.make_async_remote_copy(
        src_ref=dst, dst_ref=dst, send_sem=send, recv_sem=recv, device_id=to,
        device_id_type=pl.DeviceIdType.MESH,
    ).wait_recv()


def layer_kernel(
    x_hbm, mod, wq_hbm, wo_hbm, wu_hbm, bias, wd_hbm, guide, out,
    xa, wq, wu, wo, wd, sb, ownq, ownu, r1, r2, att, acto, pb, rb, res, acc, xs, st, mom1, mom2,
    lx, lq, lu, lo, ld, s_mom1, r_mom1, s_mom2, r_mom2, s_gat, r_gat, s_red, r_red, s_core, r_core,
    s_x, r_x, s_att, r_att,
):
    r, z = lax.axis_index("row"), lax.axis_index("col")
    core = lax.rem(r, 2)
    chunk, width = xa.shape[2], xa.shape[3]
    tokens = N * chunk
    bw = wq.shape[2]
    half = 6 * bw
    feats = 4 * width
    tile = 256 if width % 256 == 0 else 128
    mate, across, diag = {"row": r ^ 1}, {"row": r ^ 2}, {"row": r ^ 3}
    above, below = {"col": jnp.minimum(z + 1, N - 1)}, {"col": jnp.maximum(z - 1, 0)}

    local_x = pltpu.make_async_copy(x_hbm, sb.at[0, :, 0:width], lx)
    local_x.start()
    loads = {"q": [], "o": [], "u": [], "d": []}
    for i in (6, 7, 8, 9, 10, 11, 0, 1, 2, 3, 4, 5):
        owner = r ^ (0, 2, 1, 3)[i // 3]
        cols = pl.ds(pl.multiple_of(owner * bw, bw), bw)
        loads["q"].append(pltpu.make_async_copy(wq_hbm.at[i % 3, :, cols], wq.at[i], lq.at[i]))
    for i in range(4):
        owner = r ^ (0, 2, 1, 3)[i]
        rows = pl.ds(pl.multiple_of(owner * bw, bw), bw)
        loads["o"].append(pltpu.make_async_copy(wo_hbm.at[rows], wo.at[pl.ds(i * bw, bw)], lo.at[i]))
    for i in (6, 7, 8, 9, 10, 11, 0, 1, 2, 3, 4, 5):
        side = core if i < 6 else 1 - core
        cols = pl.ds(pl.multiple_of(side * half + (i % 6) * bw, bw), bw)
        loads["u"].append(pltpu.make_async_copy(wu_hbm.at[:, cols], wu.at[i], lu.at[i]))
    for i in range(2):
        side = core if i == 0 else 1 - core
        rows = pl.ds(pl.multiple_of(side * half, bw), half)
        loads["d"].append(pltpu.make_async_copy(wd_hbm.at[rows], wd.at[i], ld.at[i]))

    def ready(name, only=None):
        for i, load in enumerate(loads[name]):
            if only is None or i in only:
                load.wait()

    barrier = pltpu.get_barrier_semaphore()

    def greet(to, cond=None):
        run(cond, lambda: pl.semaphore_signal(barrier, inc=1, device_id=to, device_id_type=pl.DeviceIdType.MESH))

    for to in (mate, across, diag):
        greet(to)
    greet(above, z < N - 1)
    greet(below, z > 0)
    inner = (z > 0) & (z < N - 1)
    run(inner, lambda: pl.semaphore_wait(barrier, 5))
    run(jnp.logical_not(inner), lambda: pl.semaphore_wait(barrier, 4))

    local_x.wait()
    for group in loads.values():
        for load in group:
            load.start()

    pending = {}

    def send(key, moves):
        pending[key] = moves
        for move in moves:
            move.start()

    def settle(key):
        for move in pending.pop(key, []):
            move.wait_send()

    def stats_rows(values, into, rows):
        total = jnp.sum(values, axis=1, keepdims=True)
        squares = jnp.sum(values * values, axis=1, keepdims=True)
        lane = lax.broadcasted_iota(jnp.int32, (values.shape[0], 128), 1)
        into[rows, :] = jnp.where(lane == 0, total, squares)

    def scales(total):
        mean = total[0:1] / feats
        rstd = lax.rsqrt(total[1:2] / feats - mean * mean + eps)
        lane = lax.broadcasted_iota(jnp.int32, (128, total.shape[1]), 0)
        return jnp.where(lane == 0, mean, rstd).T

    for i in range(width // 128):
        cols = slice(i * 128, (i + 1) * 128)
        xs[i % 2] = sb[0, :, cols].astype(F32)
        for b in range(N):
            res[b, :, cols] = xs[i % 2, pl.ds(b, chunk, stride=N), :]
    for b in range(N):
        stats_rows(res[b], st, slice(b * chunk, (b + 1) * chunk))
    mom1[0] = st[...].T[0:8]
    send("mom1", [
        Move(mom1.at[0], mom1.at[m], s_mom1.at[m - 1], r_mom1.at[m - 1], to)
        for m, to in ((1, mate), (2, across), (3, diag))
    ])
    for m in (1, 2, 3):
        received(mom1.at[m], r_mom1.at[m - 1], s_mom1.at[m - 1], mate)
    st[...] = scales(mom1[0] + mom1[1] + mom1[2] + mom1[3])

    def part_rows(sizes, p, whole=chunk):
        return slice(sum(sizes[:p]) * (whole // 4), sum(sizes[: p + 1]) * (whole // 4))

    gather_sizes = (IN_PARTS, PARTS)

    def gather_start(stage, b, p):
        mine = xa.at[b, z, part_rows(gather_sizes[stage][b], p)]
        sends, gets = s_gat.at[stage, b, p], r_gat.at[stage, b, p]
        up = Move(mine, mine, sends.at[0, 0], gets.at[0, 0], above, z < N - 1)
        down = Move(mine, mine, sends.at[1, 0], gets.at[1, 0], below, z > 0)
        send(("gat", stage, b, p, 0), [up, down])

    def gather_hop(stage, b, p, h):
        low, high = jnp.maximum(z - h, 0), jnp.minimum(z + h, N - 1)
        rows = part_rows(gather_sizes[stage][b], p)
        sends, gets = s_gat.at[stage, b, p], r_gat.at[stage, b, p]
        moves = []

        def hop(side, at, here, on, to):
            data = xa.at[b, at, rows]
            run(here, lambda: received(data, gets.at[side, h - 1], sends.at[side, 0], to))
            if h < N - 1:
                move = Move(data, data, sends.at[side, h], gets.at[side, h], to, here & on)
                move.start()
                moves.append(move)

        hop(0, low, z >= h, z < N - 1, above)
        hop(1, high, z + h <= N - 1, z > 0, below)
        pending[("gat", stage, b, p, h)] = moves

    def settle_gather(stage, b):
        for p in range(len(gather_sizes[stage][b])):
            for h in range(N):
                settle(("gat", stage, b, p, h))

    def red_move(b, key, slot, rows, p, side, j):
        k = j if side == 0 else N - 1 - j
        to = below if side == 0 else above
        return pb.at[slot, k, rows], rb.at[key, side, j, rows], s_red.at[b, p, side, j], r_red.at[b, p, side, j], to

    def reduce_start(b, key, slot, rows, p):
        moves = []
        for j in range(N - 1):
            moves.append(Move(*red_move(b, key, slot, rows, p, 0, j), z == N - 1))
            moves.append(Move(*red_move(b, key, slot, rows, p, 1, j), z == 0))
        send(("red", b, p, 0), moves)

    def reduce_hop(b, key, slot, rows, p, t):
        moves = []

        def hop(side, j, valid):
            j = jnp.clip(j, 0, N - 2)
            src, dst, ss, rs, to = red_move(b, key, slot, rows, p, side, j)

            @pl.when(valid)
            def _():
                received(dst, rs, ss, to)
                k = j if side == 0 else N - 1 - j
                pb[slot, k, rows] = (pb[slot, k, rows].astype(F32) + rb[key, side, j, rows].astype(F32)).astype(BF)

            move = Move(src, dst, ss, rs, to, valid)
            move.start()
            moves.append(move)

        down, up = t - (N - 1 - z), t - z
        hop(0, down, (z < N - 1) & (down >= 0) & (down < z))
        hop(1, up, (z > 0) & (up >= 0) & (up < N - 1 - z))
        pending[("red", b, p, t)] = moves

    def reduce_end(b, key, rows, p, add):
        for side, j, valid in ((0, z, z < N - 1), (1, N - 1 - z, z > 0)):
            j = jnp.minimum(j, N - 2)

            def take(side=side, j=j):
                received(rb.at[key, side, j, rows], r_red.at[b, p, side, j], s_red.at[b, p, side, j], mate)
                add(rb[key, side, j, rows].astype(F32))

            run(valid, take)

    def settle_reduce(b):
        for p in range(MOST):
            for t in range(N - 1):
                settle(("red", b, p, t))

    order = list(ORDER)
    for b in range(N):
        sc = st[b * chunk : (b + 1) * chunk, :]
        normed = (res[b] - sc[:, 0:1]) * sc[:, 1:2]
        xa[b, z] = (normed * (1.0 + mod[1, b : b + 1, :]) + mod[0, b : b + 1, :]).astype(BF)
        while order and order[0].split("_")[0] == "A0" and int(order[0][3]) == b:
            gather_start(0, b, int(order.pop(0)[5]))

    def project(b, rows, weight, first, target):
        def body(i, carry):
            cols = pl.ds(pl.multiple_of(i * bw, bw), bw)
            left = xa[b, :, rows].reshape(-1, width)
            target[:, cols] = jnp.dot(left, weight[first + i], preferred_element_type=F32).astype(BF)
            return carry

        lax.fori_loop(0, 6, body, 0, unroll=True)

    def project_all(kind, b, p, rows, span, s, weight, own, name):
        first = (b, p) == (0, 0)
        settle(("core", s))
        if first:
            ready(name, range(6))
        project(b, rows, weight, 6, sb.at[s, span])
        send(("core", s), [
            Move(sb.at[s, span], r1.at[b, span], s_core.at[kind, b, p], r_core.at[kind, b, p], mate)])
        if first:
            ready(name, range(6, 12))
        for old in range(MOST):
            if p == 0 or kind:
                settle(("own", kind, s, old))
        project(b, rows, weight, 0, own.at[s, span])

    def pair_sum(own, s, b, span, cols):
        own[s, span, cols] = (own[s, span, cols].astype(F32) + r1[b, span, cols].astype(F32)).astype(BF)

    def do_A(h, b, p):
        if h == 0:
            gather_start(0, b, p)
        else:
            gather_hop(0, b, p, h)

    def q_parts(b):
        if not Q_SPLIT[b]:
            return [(slice(0, chunk), slice(0, tokens))]
        sizes = IN_PARTS[b]
        return [(part_rows(sizes, p), part_rows(sizes, p, tokens)) for p in range(len(sizes))]

    def do_Q1(b, p):
        rows, span = q_parts(b)[p]
        project_all(0, b, p, rows, span, b % 2, wq, ownq, "q")

    def q_move(b, p):
        span = q_parts(b)[p][1]
        return Move(
            ownq.at[b % 2, span, 3 * bw : half], r2.at[b, span, 0 : 3 * bw], s_x.at[0, b, p], r_x.at[0, b, p], across)

    def do_Q2(b, p):
        span = q_parts(b)[p][1]
        received(r1.at[b, span], r_core.at[0, b, p], s_core.at[0, b, p], mate)
        for i in range(3, 6):
            pair_sum(ownq, b % 2, b, span, slice(i * bw, (i + 1) * bw))
        send(("own", 0, b % 2, p), [q_move(b, p)])

    def do_T1(b):
        for p, (_, span) in enumerate(q_parts(b)):
            received(r2.at[b, span, 0 : 3 * bw], r_x.at[0, b, p], s_x.at[0, b, p], across)
        qkv = []
        for j in range(3):
            cols = slice(j * bw, (j + 1) * bw)
            total = ownq[b % 2, :, cols].astype(F32) + r1[b, :, cols].astype(F32) + r2[b, :, cols].astype(F32)
            qkv.append(total.astype(BF))
        for h in range(bw // HEAD_DIM):
            cols = slice(h * HEAD_DIM, (h + 1) * HEAD_DIM)
            scores = lax.dot_general(
                qkv[0][:, cols], qkv[1][:, cols], (((1,), (1,)), ((), ())), preferred_element_type=F32)
            scores = scores * (1.0 / HEAD_DIM**0.5)
            weights = jnp.exp(scores - jnp.max(scores, axis=-1, keepdims=True))
            denom = jnp.sum(weights, axis=-1, keepdims=True)
            mixed = jnp.dot(weights.astype(BF), qkv[2][:, cols], preferred_element_type=F32)
            att[b, :, cols] = (mixed / denom).astype(BF)
        send(("att", b, 0), [
            Move(att.at[b, :, 0:bw], att.at[b, :, bw : 2 * bw], s_att.at[b, 0], r_att.at[b, 0], across),
            Move(att.at[b, :, 0:bw], att.at[b, :, 2 * bw : 3 * bw], s_att.at[b, 1], r_att.at[b, 1], mate),
        ])

    def do_T2(b):
        received(att.at[b, :, bw : 2 * bw], r_att.at[b, 0], s_att.at[b, 0], across)
        send(("att", b, 1), [
            Move(att.at[b, :, bw : 2 * bw], att.at[b, :, 3 * bw : 4 * bw], s_att.at[b, 2], r_att.at[b, 2], mate)])

    def do_O(b):
        received(att.at[b, :, 2 * bw : 3 * bw], r_att.at[b, 1], s_att.at[b, 1], mate)
        received(att.at[b, :, 3 * bw : 4 * bw], r_att.at[b, 2], s_att.at[b, 2], mate)
        if b == 0:
            ready("o")
        if b >= 2:
            settle_reduce(b - 2)
        settle_gather(0, b)

        def body(i, carry):
            cols = pl.ds(pl.multiple_of(i * tile, tile), tile)
            part = jnp.dot(att[b], wo[:, cols], preferred_element_type=F32).astype(BF)
            for rows, span in q_parts(b):
                pb[b % 2, :, rows, cols] = part[span].reshape(N, -1, tile)
            return carry

        lax.fori_loop(0, width // tile, body, 0, unroll=True)
        for p in range(len(PARTS[b])):
            reduce_start(b, b, b % 2, part_rows(PARTS[b], p), p)

    def do_B(t, b, p):
        reduce_hop(b, b, b % 2, part_rows(PARTS[b], p), p, t)

    def do_N1(b, p):
        gate, rows = mod[2, b : b + 1, :], part_rows(PARTS[b], p)
        res[b, rows] = res[b, rows] + gate * pb[b % 2, z, rows].astype(F32)

        def add(part):
            res[b, rows] = res[b, rows] + gate * part

        reduce_end(b, b, rows, p, add)
        stats_rows(res[b, rows], st, slice(0, rows.stop - rows.start))
        mom2[b, p, 0] = st[0:128, :].T[0:8]
        send(("mom2", b, p), [
            Move(mom2.at[b, p, 0], mom2.at[b, p, m], s_mom2.at[b, p, m - 1], r_mom2.at[b, p, m - 1], to)
            for m, to in ((1, mate), (2, across), (3, diag))
        ])

    def do_N2(b, p):
        rows = part_rows(PARTS[b], p)
        for m in (1, 2, 3):
            received(mom2.at[b, p, m], r_mom2.at[b, p, m - 1], s_mom2.at[b, p, m - 1], mate)
        total = mom2[b, p, 0] + mom2[b, p, 1] + mom2[b, p, 2] + mom2[b, p, 3]
        sc = scales(total)[0 : rows.stop - rows.start]
        normed = (res[b, rows] - sc[:, 0:1]) * sc[:, 1:2]
        xa[b, z, rows] = (normed * (1.0 + mod[4, b : b + 1, :]) + mod[3, b : b + 1, :]).astype(BF)

    def do_C(h, b, p):
        if h == 0:
            gather_start(1, b, p)
        else:
            gather_hop(1, b, p, h)

    units = [(b, q) for b in range(N) for q in range(len(PARTS[b]))]

    def unit(b, q):
        return units.index((b, q)) % 2, part_rows(PARTS[b], q), part_rows(PARTS[b], q, tokens)

    def do_U1(b, q):
        s, rows, span = unit(b, q)
        project_all(1, b, q, rows, span, s, wu, ownu, "u")

    def up_move(b, q, part):
        s, _, span = unit(b, q)
        cols = slice(part * 3 * bw, (part + 1) * 3 * bw)
        sem = 1 + part
        return Move(ownu.at[s, span, cols], r2.at[b, span, cols], s_x.at[sem, b, q], r_x.at[sem, b, q], across)

    def do_U(b, q, part):
        s, _, span = unit(b, q)
        if part == 0:
            received(r1.at[b, span], r_core.at[1, b, q], s_core.at[1, b, q], mate)
        for i in range(3 * part, 3 * part + 3):
            pair_sum(ownu, s, b, span, slice(i * bw, (i + 1) * bw))
        send(("ux", b, q, part), [up_move(b, q, part)])

    def do_G(b, q):
        s, _, span = unit(b, q)
        for part in range(2):
            settle(("ux", b, q, part))
            up_move(b, q, part).copy.wait_recv()

        def body(i, carry):
            cols = pl.ds(pl.multiple_of(i * bw, bw), bw)
            up = ownu[s, span, cols].astype(F32) + r2[b, span, cols].astype(F32)
            up = up + bias[:, pl.ds(pl.multiple_of(core * half + i * bw, bw), bw)]
            ownu[s, span, cols] = jax.nn.gelu(up, approximate=True).astype(BF)
            return carry

        lax.fori_loop(0, 6, body, 0)
        send(("own", 1, s, q), [
            Move(ownu.at[s, span], acto.at[b, span], s_core.at[2, b, q], r_core.at[2, b, q], mate)])

    def do_W(b, q):
        s, rows, span = unit(b, q)
        received(acto.at[b, span], r_core.at[2, b, q], s_core.at[2, b, q], mate)
        if (b, q) == (0, 0):
            ready("d")
        scale = guide[b].astype(F32) * 0.25

        def body(i, carry):
            cols = pl.ds(pl.multiple_of(i * tile, tile), tile)
            down = jnp.dot(ownu[s, span], wd[0, :, cols], preferred_element_type=F32)
            down = down + jnp.dot(acto[b, span], wd[1, :, cols], preferred_element_type=F32)
            down = (down * (mod[5, b : b + 1, cols] * scale)).reshape(N, -1, tile)
            acc[:, rows, cols] = down if b == 0 else acc[:, rows, cols] + down
            return carry

        lax.fori_loop(0, width // tile, body, 0, unroll=True)

    def do_D(t, q):
        rows = part_rows(PARTS[N - 1], q)
        if t == 0:
            settle_reduce(2)
            pb[0, :, rows] = acc[:, rows].astype(BF)
            reduce_start(N, 0, 0, rows, q)
        elif t < N - 1:
            reduce_hop(N, 0, 0, rows, q, t)
        else:
            total = acc[z, rows]
            for b in range(N):
                total = total + (guide[b].astype(F32) * 0.25) * res[b, rows]
            acc[z, rows] = total

            def finish(part):
                acc[z, rows] = acc[z, rows] + part

            reduce_end(N, 0, rows, q, finish)
            out[rows] = acc[z, rows].astype(BF)

    for event in order:
        name, where = event.split("_")
        args = [int(v) for v in where.split(".")]
        if name[0] in "ABCD":
            {"A": do_A, "B": do_B, "C": do_C, "D": do_D}[name[0]](int(name[1]), *args)
        elif name in ("U2", "U3"):
            do_U(*args, int(name[1]) - 2)
        else:
            {"Q1": do_Q1, "Q2": do_Q2, "T1": do_T1, "T2": do_T2, "O": do_O, "N1": do_N1, "N2": do_N2,
             "U1": do_U1, "G": do_G, "W": do_W}[name](*args)
    for key in list(pending):
        settle(key)


def fused_layer(clip_tokens, modulation, w_qkv, w_out, w_up, up_bias, w_down, guide_num):
    rows, width = clip_tokens.shape
    chunk = rows // N
    heads = w_qkv.shape[2]
    bw = heads // 4
    half = 6 * bw
    dma, vmem, anywhere = pltpu.SemaphoreType.DMA, pltpu.VMEM, pl.BlockSpec(memory_space=pl.ANY)
    inside = pl.BlockSpec(memory_space=pltpu.VMEM)
    scratch = [
        vmem((N, N, chunk, width), BF),
        vmem((12, width, bw), BF),
        vmem((12, width, bw), BF),
        vmem((heads, width), BF),
        vmem((2, half, width), BF),
        vmem((2, rows, half), BF),
        vmem((2, rows, half), BF),
        vmem((2, rows, half), BF),
        vmem((N, rows, half), BF),
        vmem((N, rows, half), BF),
        vmem((N, rows, heads), BF),
        vmem((N, rows, half), BF),
        vmem((2, N, chunk, width), BF),
        vmem((N, 2, N - 1, chunk, width), BF),
        vmem((N, chunk, width), F32),
        vmem((N, chunk, width), F32),
        vmem((2, rows, 128), F32),
        vmem((max(rows, 128), 128), F32),
        vmem((N, 8, max(rows, 128)), F32),
        vmem((N, MOST, N, 8, 128), F32),
        dma, dma((12,)), dma((12,)), dma((4,)), dma((2,)),
        dma((3,)), dma((3,)), dma((N, MOST, 3)), dma((N, MOST, 3)),
        dma((2, N, MOST, 2, N - 1)), dma((2, N, MOST, 2, N - 1)),
        dma((N + 1, MOST, 2, N - 1)), dma((N + 1, MOST, 2, N - 1)),
        dma((3, N, MOST)), dma((3, N, MOST)), dma((3, N, MOST)), dma((3, N, MOST)), dma((N, 3)), dma((N, 3)),
    ]
    return pl.pallas_call(
        layer_kernel,
        out_shape=jax.ShapeDtypeStruct((chunk, width), BF),
        in_specs=[anywhere, inside, anywhere, anywhere, anywhere, inside, anywhere,
                  pl.BlockSpec(memory_space=pltpu.SMEM)],
        out_specs=inside,
        scratch_shapes=scratch,
        compiler_params=pltpu.CompilerParams(
            collective_id=0, has_side_effects=True, vmem_limit_bytes=121 * 512 * 1024),
    )(
        clip_tokens, modulation.transpose(1, 0, 2), w_qkv.transpose(1, 0, 2), w_out, w_up,
        up_bias[None], w_down, guide_num,
    )


def on_device(*args):
    tokens, modulation, w_qkv, _, w_up = args[:5]
    head_cols = w_qkv.shape[2]
    square = lax.axis_size("row") == 4 and lax.axis_size("col") == 4 and modulation.shape[0] == 4
    if square and head_cols % 512 == 0 and w_up.shape[1] == 3 * head_cols and tokens.shape[0] % 128 == 0:
        return fused_layer(*args)
    return general_layer(*args)


def solution(mesh):
    in_specs = (
        P(("clips", "col"), "row"),
        P("clips", None, "row"),
        P("row", None, "col"),
        P("col", "row"),
        P("row", "col"),
        P("col"),
        P("col", "row"),
        P("clips"),
    )
    out_specs = P(("clips", "col"), "row")
    return jax.shard_map(
        on_device, mesh=mesh, in_specs=in_specs, out_specs=out_specs, check_vma=False
    )
```

```python
import functools

import jax
import jax.numpy as jnp
from jax import lax
from jax.experimental import pallas as pl
from jax.experimental.pallas import tpu as pltpu
from jax.sharding import PartitionSpec as P

HEAD_DIM = 128
BF = jnp.bfloat16
F32 = jnp.float32
eps = 1e-06
N = 4
IN_PARTS = ((1, 3), (1, 3), (2, 2), (4,))
Q_SPLIT = (1, 1, 1, 1)
PARTS = ((2, 2), (2, 2), (2, 2), (2, 2))
MOST = 3
UNROLL = 3
KINDS = (
    "A0", "A1", "A2", "A3", "Q1", "Q2", "T1", "T2", "O", "B1", "B2", "N1", "N2", "C0", "C1", "C2", "C3",
    "U1", "U2", "U3", "G", "W", "D0", "D1", "D2", "D3",
)
ORDER = (
    0, 1, 16, 4, 17, 32, 20, 48, 64, 33, 5, 8, 80, 49, 65, 81, 36, 52, 21, 68,
    84, 37, 24, 9, 96, 53, 69, 40, 12, 85, 25, 112, 128, 56, 72, 100, 41, 28, 57, 144,
    73, 88, 116, 132, 89, 44, 145, 60, 160, 76, 161, 148, 176, 104, 192, 208, 164, 177, 92, 120,
    149, 193, 209, 136, 180, 224, 165, 240, 225, 152, 108, 181, 196, 212, 256, 272, 241, 153, 288, 124,
    168, 304, 197, 213, 257, 140, 273, 228, 169, 184, 289, 305, 244, 229, 320, 200, 156, 216, 336, 260,
    276, 185, 292, 245, 172, 308, 321, 157, 201, 337, 261, 232, 277, 217, 293, 188, 248, 309, 324, 173,
    233, 340, 264, 280, 204, 220, 296, 249, 325, 189, 236, 312, 341, 265, 281, 252, 297, 205, 313, 221,
    328, 268, 344, 237, 284, 300, 253, 329, 316, 345, 269, 285, 301, 332, 317, 348, 352, 368, 333, 384,
    349, 353, 369, 400, 385, 401,
)


def normalize(values, shift, scale):
    totals = lax.psum((jnp.sum(values, axis=1), jnp.sum(values * values, axis=1)), "row")
    width = values.shape[1] * lax.axis_size("row")
    mean = totals[0] / width
    variance = totals[1] / width - mean * mean
    normed = (values - mean[:, None]) * lax.rsqrt(variance + eps)[:, None]
    branches = shift.shape[0]
    shaped = normed.reshape(-1, branches, values.shape[1]) * (1.0 + scale[None]) + shift[None]
    return shaped.reshape(values.shape)


def general_layer(clip_tokens, modulation, w_qkv, w_out, w_up, up_bias, w_down, guide_num):
    branches = modulation.shape[0]
    feat_rows = w_qkv.shape[0]
    head_cols = w_qkv.shape[2]
    heads_here = head_cols // HEAD_DIM
    x_rows = clip_tokens.astype(jnp.float32)
    first = normalize(x_rows, modulation[:, 0], modulation[:, 1]).astype(jnp.bfloat16)
    w_flat = w_qkv.reshape(feat_rows, 3 * head_cols)
    partial_qkv = jnp.dot(
        lax.all_gather(first, "col", axis=0, tiled=True), w_flat, preferred_element_type=jnp.float32
    )
    scale_score = 1.0 / jnp.sqrt(jnp.float32(HEAD_DIM))
    qkv = lax.psum_scatter(partial_qkv.astype(jnp.bfloat16), "row", scatter_dimension=0, tiled=True)
    query3 = qkv[:, :head_cols].reshape(-1, heads_here, HEAD_DIM)
    query_rows = query3.shape[0]
    piece = (
        lax.all_gather(qkv[:, head_cols : 2 * head_cols], "row", axis=0, tiled=True),
        lax.all_gather(qkv[:, 2 * head_cols :], "row", axis=0, tiled=True),
    )
    top = jnp.full((heads_here, query_rows), -1e30, jnp.float32)
    rows = piece[0].shape[0]
    key_heads = piece[0].reshape(rows, heads_here, HEAD_DIM)
    value_heads = piece[1].reshape(rows, heads_here, HEAD_DIM)
    scores = (
        jnp.einsum("qhd,khd->hqk", query3, key_heads, preferred_element_type=jnp.float32)
        * scale_score
    )
    query_branch = jnp.arange(query3.shape[0], dtype=jnp.int32) % branches
    key_branch = jnp.arange(rows, dtype=jnp.int32) % branches
    allowed = (query_branch[:, None] == key_branch[None, :])[None]
    masked = jnp.where(allowed, scores, -1e30)
    new_top = jnp.maximum(top, jnp.max(masked, axis=-1))
    weights = jnp.where(allowed, jnp.exp(masked - new_top[..., None]), 0.0)
    denom = jnp.sum(weights, axis=-1)
    accum = jnp.einsum(
        "hqk,khd->hqd",
        weights.astype(jnp.bfloat16),
        value_heads,
        preferred_element_type=jnp.float32,
    )
    att = (accum / denom[..., None]).transpose(1, 0, 2).reshape(-1, head_cols).astype(jnp.bfloat16)
    partial_out = jnp.dot(
        lax.all_gather(att, "row", axis=0, tiled=True), w_out, preferred_element_type=jnp.float32
    )
    out_rows = lax.psum_scatter(
        partial_out.astype(jnp.bfloat16), "col", scatter_dimension=0, tiled=True
    ).astype(jnp.float32)
    by_branch = x_rows.shape[0] // branches
    resid = (
        x_rows.reshape(by_branch, branches, feat_rows)
        + modulation[None, :, 2] * out_rows.reshape(by_branch, branches, feat_rows)
    ).reshape(x_rows.shape)
    second = normalize(resid, modulation[:, 3], modulation[:, 4]).astype(jnp.bfloat16)
    partial_up = jnp.dot(
        lax.all_gather(second, "col", axis=0, tiled=True), w_up, preferred_element_type=jnp.float32
    )
    up_rows = lax.psum_scatter(
        partial_up.astype(jnp.bfloat16), "row", scatter_dimension=0, tiled=True
    ).astype(jnp.float32)
    act = jax.nn.gelu(up_rows + up_bias[None], approximate=True).astype(jnp.bfloat16)
    partial_down = jnp.dot(
        lax.all_gather(act, "row", axis=0, tiled=True), w_down, preferred_element_type=jnp.float32
    )
    guide_weights = guide_num.astype(jnp.float32) / 4.0
    weights_gate = guide_weights[:, None] * modulation[:, 5]
    combined = jnp.sum(partial_down.reshape(-1, branches, feat_rows) * weights_gate[None], axis=1)
    mlp_rows = lax.psum_scatter(
        combined.astype(jnp.bfloat16), "col", scatter_dimension=0, tiled=True
    ).astype(jnp.float32)
    resid_mix = jnp.sum(
        resid.reshape(by_branch, branches, feat_rows) * guide_weights[None, :, None], axis=1
    )
    return (resid_mix + mlp_rows).astype(jnp.bfloat16)


class Move:
    def __init__(self, src, dst, send, recv, to, sent=None, got=None):
        self.copy = pltpu.make_async_remote_copy(
            src_ref=src, dst_ref=dst, send_sem=send, recv_sem=recv, device_id=to,
            device_id_type=pl.DeviceIdType.MESH,
        )
        self.sent = sent

    def start(self):
        run(self.sent, self.copy.start)

    def wait_send(self):
        run(self.sent, self.copy.wait_send)


def run(cond, act):
    if cond is None:
        act()
    else:
        pl.when(cond)(lambda: act() and None)


def received(dst, recv, send, to):
    pltpu.make_async_remote_copy(
        src_ref=dst, dst_ref=dst, send_sem=send, recv_sem=recv, device_id=to,
        device_id_type=pl.DeviceIdType.MESH,
    ).wait_recv()


def layer_kernel(
    x_hbm, mod, wq_hbm, wo_hbm, wu_hbm, bias, wd_hbm, guide, out,
    xa, wq, wu, wo, wd, work, r1, r2, att, acto, pb, rb, res, acc, xs, st, mom1, mom2,
    lx, lq, lu, lo, ld, s_mom1, r_mom1, s_mom2, r_mom2, s_gat, r_gat, s_red, r_red, s_core, r_core,
    s_x, r_x, s_att, r_att,
):
    r, z = lax.axis_index("row"), lax.axis_index("col")
    core = lax.rem(r, 2)
    chunk, width = xa.shape[2], xa.shape[3]
    sb, ownq, ownu = work.at[0:2], work.at[2:4], work.at[4:6]
    tokens = N * chunk
    bw = wq.shape[2]
    half = 6 * bw
    feats = 4 * width
    tile = 256 if width % 256 == 0 else 128
    mate, across, diag = {"row": r ^ 1}, {"row": r ^ 2}, {"row": r ^ 3}
    above, below = {"col": jnp.minimum(z + 1, N - 1)}, {"col": jnp.maximum(z - 1, 0)}

    local_x = pltpu.make_async_copy(x_hbm, sb.at[0, :, 0:width], lx)
    local_x.start()
    loads = {"q": [], "o": [], "u": [], "d": []}
    for i in (6, 7, 8, 9, 10, 11, 0, 1, 2, 3, 4, 5):
        owner = r ^ (0, 2, 1, 3)[i // 3]
        cols = pl.ds(pl.multiple_of(owner * bw, bw), bw)
        loads["q"].append(pltpu.make_async_copy(wq_hbm.at[i % 3, :, cols], wq.at[i], lq.at[i]))
    for i in range(4):
        owner = r ^ (0, 2, 1, 3)[i]
        rows = pl.ds(pl.multiple_of(owner * bw, bw), bw)
        loads["o"].append(pltpu.make_async_copy(wo_hbm.at[rows], wo.at[pl.ds(i * bw, bw)], lo.at[i]))
    for i in (6, 7, 8, 9, 10, 11, 0, 1, 2, 3, 4, 5):
        side = core if i < 6 else 1 - core
        cols = pl.ds(pl.multiple_of(side * half + (i % 6) * bw, bw), bw)
        loads["u"].append(pltpu.make_async_copy(wu_hbm.at[:, cols], wu.at[i], lu.at[i]))
    for i in range(2):
        side = core if i == 0 else 1 - core
        rows = pl.ds(pl.multiple_of(side * half, bw), half)
        loads["d"].append(pltpu.make_async_copy(wd_hbm.at[rows], wd.at[i], ld.at[i]))

    def ready(name, only=None):
        for i, load in enumerate(loads[name]):
            if only is None or i in only:
                load.wait()

    barrier = pltpu.get_barrier_semaphore()

    def greet(to, cond=None):
        run(cond, lambda: pl.semaphore_signal(barrier, inc=1, device_id=to, device_id_type=pl.DeviceIdType.MESH))

    for to in (mate, across, diag):
        greet(to)
    greet(above, z < N - 1)
    greet(below, z > 0)
    inner = (z > 0) & (z < N - 1)
    run(inner, lambda: pl.semaphore_wait(barrier, 5))
    run(jnp.logical_not(inner), lambda: pl.semaphore_wait(barrier, 4))

    local_x.wait()
    for group in loads.values():
        for load in group:
            load.start()

    pending = {}

    def send(key, moves):
        pending[key] = moves
        for move in moves:
            move.start()

    def settle(key):
        for move in pending.pop(key, []):
            move.wait_send()

    def stats_rows(values, into, rows):
        total = jnp.sum(values, axis=1, keepdims=True)
        squares = jnp.sum(values * values, axis=1, keepdims=True)
        lane = lax.broadcasted_iota(jnp.int32, (values.shape[0], 128), 1)
        into[rows, :] = jnp.where(lane == 0, total, squares)

    def scales(total):
        mean = total[0:1] / feats
        rstd = lax.rsqrt(total[1:2] / feats - mean * mean + eps)
        lane = lax.broadcasted_iota(jnp.int32, (128, total.shape[1]), 0)
        return jnp.where(lane == 0, mean, rstd).T

    for i in range(width // 128):
        cols = slice(i * 128, (i + 1) * 128)
        xs[i % 2] = sb[0, :, cols].astype(F32)
        for b in range(N):
            res[b, :, cols] = xs[i % 2, pl.ds(b, chunk, stride=N), :]
    for b in range(N):
        stats_rows(res[b], st, slice(b * chunk, (b + 1) * chunk))
    mom1[0] = st[...].T[0:8]
    send("mom1", [
        Move(mom1.at[0], mom1.at[m], s_mom1.at[m - 1], r_mom1.at[m - 1], to)
        for m, to in ((1, mate), (2, across), (3, diag))
    ])
    for m in (1, 2, 3):
        received(mom1.at[m], r_mom1.at[m - 1], s_mom1.at[m - 1], mate)
    st[...] = scales(mom1[0] + mom1[1] + mom1[2] + mom1[3])

    def part_rows(sizes, p, whole=chunk):
        return slice(sum(sizes[:p]) * (whole // 4), sum(sizes[: p + 1]) * (whole // 4))

    gather_sizes = (IN_PARTS, PARTS)

    def gather_start(stage, b, p):
        mine = xa.at[b, z, part_rows(gather_sizes[stage][b], p)]
        sends, gets = s_gat.at[stage, b, p], r_gat.at[stage, b, p]
        up = Move(mine, mine, sends.at[0, 0], gets.at[0, 0], above, z < N - 1)
        down = Move(mine, mine, sends.at[1, 0], gets.at[1, 0], below, z > 0)
        send(("gat", stage, b, p, 0), [up, down])

    def gather_hop(stage, b, p, h):
        low, high = jnp.maximum(z - h, 0), jnp.minimum(z + h, N - 1)
        rows = part_rows(gather_sizes[stage][b], p)
        sends, gets = s_gat.at[stage, b, p], r_gat.at[stage, b, p]
        moves = []

        def hop(side, at, here, on, to):
            data = xa.at[b, at, rows]
            run(here, lambda: received(data, gets.at[side, h - 1], sends.at[side, 0], to))
            if h < N - 1:
                move = Move(data, data, sends.at[side, h], gets.at[side, h], to, here & on)
                move.start()
                moves.append(move)

        hop(0, low, z >= h, z < N - 1, above)
        hop(1, high, z + h <= N - 1, z > 0, below)
        pending[("gat", stage, b, p, h)] = moves

    def settle_gather(stage, b):
        for p in range(len(gather_sizes[stage][b])):
            for h in range(N):
                settle(("gat", stage, b, p, h))

    def red_move(b, key, slot, rows, p, side, j):
        k = j if side == 0 else N - 1 - j
        to = below if side == 0 else above
        return pb.at[slot, k, rows], rb.at[key, side, j, rows], s_red.at[b, p, side, j], r_red.at[b, p, side, j], to

    def reduce_start(b, key, slot, rows, p):
        moves = []
        for j in range(N - 1):
            moves.append(Move(*red_move(b, key, slot, rows, p, 0, j), z == N - 1))
            moves.append(Move(*red_move(b, key, slot, rows, p, 1, j), z == 0))
        send(("red", b, p, 0), moves)

    def reduce_hop(b, key, slot, rows, p, t):
        moves = []

        def hop(side, j, valid):
            j = jnp.clip(j, 0, N - 2)
            src, dst, ss, rs, to = red_move(b, key, slot, rows, p, side, j)

            @pl.when(valid)
            def _():
                received(dst, rs, ss, to)
                k = j if side == 0 else N - 1 - j
                pb[slot, k, rows] = (pb[slot, k, rows].astype(F32) + rb[key, side, j, rows].astype(F32)).astype(BF)

            move = Move(src, dst, ss, rs, to, valid)
            move.start()
            moves.append(move)

        down, up = t - (N - 1 - z), t - z
        hop(0, down, (z < N - 1) & (down >= 0) & (down < z))
        hop(1, up, (z > 0) & (up >= 0) & (up < N - 1 - z))
        pending[("red", b, p, t)] = moves

    def reduce_end(b, key, rows, p, add):
        for side, j, valid in ((0, z, z < N - 1), (1, N - 1 - z, z > 0)):
            j = jnp.minimum(j, N - 2)

            def take(side=side, j=j):
                received(rb.at[key, side, j, rows], r_red.at[b, p, side, j], s_red.at[b, p, side, j], mate)
                add(rb[key, side, j, rows].astype(F32))

            run(valid, take)

    def settle_reduce(b):
        for p in range(MOST):
            for t in range(N - 1):
                settle(("red", b, p, t))

    order = list(ORDER)
    for b in range(N):
        sc = st[b * chunk : (b + 1) * chunk, :]
        normed = (res[b] - sc[:, 0:1]) * sc[:, 1:2]
        xa[b, z] = (normed * (1.0 + mod[1, b : b + 1, :]) + mod[0, b : b + 1, :]).astype(BF)
        while order[0] < 16 and order[0] // 4 == b:
            gather_start(0, b, order.pop(0) % 4)

    def project_all(kind, b, p, rows, span, s, weight, name):
        settle(("core", s))
        if (b, p) == (0, 0):
            ready(name)
        for old in range(MOST):
            if p == 0 or kind:
                settle(("own", kind, s, old))
        away = Move(sb.at[s, span], r1.at[b, span], s_core.at[kind, b, p], r_core.at[kind, b, p], mate)

        def body(g, carry):
            pl.when(g == 1)(lambda: away.start())
            slot = jnp.where(g == 0, s, 2 + 2 * kind + s)
            left = xa[b, :, rows].reshape(-1, width)
            for k in range(6):
                part = jnp.dot(left, weight[6 * (1 - g) + k], preferred_element_type=F32)
                work[slot, span, k * bw : (k + 1) * bw] = part.astype(BF)
            return carry

        lax.fori_loop(0, 2, body, 0)
        pending[("core", s)] = [away]

    def pair_sum(own, s, b, span, cols):
        own[s, span, cols] = (own[s, span, cols].astype(F32) + r1[b, span, cols].astype(F32)).astype(BF)

    def do_A(h, b, p):
        if h == 0:
            gather_start(0, b, p)
        else:
            gather_hop(0, b, p, h)

    def q_parts(b):
        if not Q_SPLIT[b]:
            return [(slice(0, chunk), slice(0, tokens))]
        sizes = IN_PARTS[b]
        return [(part_rows(sizes, p), part_rows(sizes, p, tokens)) for p in range(len(sizes))]

    def do_Q1(b, p):
        rows, span = q_parts(b)[p]
        project_all(0, b, p, rows, span, b % 2, wq, "q")

    def q_move(b, p):
        span = q_parts(b)[p][1]
        return Move(
            ownq.at[b % 2, span, 3 * bw : half], r2.at[b, span, 0 : 3 * bw], s_x.at[0, b, p], r_x.at[0, b, p], across)

    def do_Q2(b, p):
        span = q_parts(b)[p][1]
        received(r1.at[b, span], r_core.at[0, b, p], s_core.at[0, b, p], mate)
        for i in range(3, 6):
            pair_sum(ownq, b % 2, b, span, slice(i * bw, (i + 1) * bw))
        send(("own", 0, b % 2, p), [q_move(b, p)])

    def do_T1(b):
        for p, (_, span) in enumerate(q_parts(b)):
            received(r2.at[b, span, 0 : 3 * bw], r_x.at[0, b, p], s_x.at[0, b, p], across)
        qkv = []
        for j in range(3):
            cols = slice(j * bw, (j + 1) * bw)
            total = ownq[b % 2, :, cols].astype(F32) + r1[b, :, cols].astype(F32) + r2[b, :, cols].astype(F32)
            qkv.append(total.astype(BF))
        for h in range(bw // HEAD_DIM):
            cols = slice(h * HEAD_DIM, (h + 1) * HEAD_DIM)
            scores = lax.dot_general(
                qkv[0][:, cols], qkv[1][:, cols], (((1,), (1,)), ((), ())), preferred_element_type=F32)
            scores = scores * (1.0 / HEAD_DIM**0.5)
            weights = jnp.exp(scores - jnp.max(scores, axis=-1, keepdims=True))
            denom = jnp.sum(weights, axis=-1, keepdims=True)
            mixed = jnp.dot(weights.astype(BF), qkv[2][:, cols], preferred_element_type=F32)
            att[b, :, cols] = (mixed / denom).astype(BF)
        send(("att", b, 0), [
            Move(att.at[b, :, 0:bw], att.at[b, :, bw : 2 * bw], s_att.at[b, 0], r_att.at[b, 0], across),
            Move(att.at[b, :, 0:bw], att.at[b, :, 2 * bw : 3 * bw], s_att.at[b, 1], r_att.at[b, 1], mate),
        ])

    def do_T2(b):
        received(att.at[b, :, bw : 2 * bw], r_att.at[b, 0], s_att.at[b, 0], across)
        send(("att", b, 1), [
            Move(att.at[b, :, bw : 2 * bw], att.at[b, :, 3 * bw : 4 * bw], s_att.at[b, 2], r_att.at[b, 2], mate)])

    def do_O(b):
        received(att.at[b, :, 2 * bw : 3 * bw], r_att.at[b, 1], s_att.at[b, 1], mate)
        received(att.at[b, :, 3 * bw : 4 * bw], r_att.at[b, 2], s_att.at[b, 2], mate)
        if b == 0:
            ready("o")
        if b >= 2:
            settle_reduce(b - 2)
        settle_gather(0, b)

        def body(i, carry):
            cols = pl.ds(pl.multiple_of(i * tile, tile), tile)
            part = jnp.dot(att[b], wo[:, cols], preferred_element_type=F32).astype(BF)
            for rows, span in q_parts(b):
                pb[b % 2, :, rows, cols] = part[span].reshape(N, -1, tile)
            return carry

        lax.fori_loop(0, width // tile, body, 0, unroll=UNROLL)
        for p in range(len(PARTS[b])):
            reduce_start(b, b, b % 2, part_rows(PARTS[b], p), p)

    def do_B(t, b, p):
        reduce_hop(b, b, b % 2, part_rows(PARTS[b], p), p, t)

    def do_N1(b, p):
        gate, rows = mod[2, b : b + 1, :], part_rows(PARTS[b], p)
        res[b, rows] = res[b, rows] + gate * pb[b % 2, z, rows].astype(F32)

        def add(part):
            res[b, rows] = res[b, rows] + gate * part

        reduce_end(b, b, rows, p, add)
        stats_rows(res[b, rows], st, slice(0, rows.stop - rows.start))
        mom2[b, p, 0] = st[0:128, :].T[0:8]
        send(("mom2", b, p), [
            Move(mom2.at[b, p, 0], mom2.at[b, p, m], s_mom2.at[b, p, m - 1], r_mom2.at[b, p, m - 1], to)
            for m, to in ((1, mate), (2, across), (3, diag))
        ])

    def do_N2(b, p):
        rows = part_rows(PARTS[b], p)
        for m in (1, 2, 3):
            received(mom2.at[b, p, m], r_mom2.at[b, p, m - 1], s_mom2.at[b, p, m - 1], mate)
        total = mom2[b, p, 0] + mom2[b, p, 1] + mom2[b, p, 2] + mom2[b, p, 3]
        sc = scales(total)[0 : rows.stop - rows.start]
        normed = (res[b, rows] - sc[:, 0:1]) * sc[:, 1:2]
        xa[b, z, rows] = (normed * (1.0 + mod[4, b : b + 1, :]) + mod[3, b : b + 1, :]).astype(BF)

    def do_C(h, b, p):
        if h == 0:
            gather_start(1, b, p)
        else:
            gather_hop(1, b, p, h)

    units = [(b, q) for b in range(N) for q in range(len(PARTS[b]))]

    def unit(b, q):
        return units.index((b, q)) % 2, part_rows(PARTS[b], q), part_rows(PARTS[b], q, tokens)

    def do_U1(b, q):
        s, rows, span = unit(b, q)
        project_all(1, b, q, rows, span, s, wu, "u")

    def up_move(b, q, part):
        s, _, span = unit(b, q)
        cols = slice(part * 3 * bw, (part + 1) * 3 * bw)
        sem = 1 + part
        return Move(ownu.at[s, span, cols], r2.at[b, span, cols], s_x.at[sem, b, q], r_x.at[sem, b, q], across)

    def do_U(b, q, part):
        s, _, span = unit(b, q)
        if part == 0:
            received(r1.at[b, span], r_core.at[1, b, q], s_core.at[1, b, q], mate)
        for i in range(3 * part, 3 * part + 3):
            pair_sum(ownu, s, b, span, slice(i * bw, (i + 1) * bw))
        send(("ux", b, q, part), [up_move(b, q, part)])

    def do_G(b, q):
        s, _, span = unit(b, q)
        for part in range(2):
            settle(("ux", b, q, part))
            up_move(b, q, part).copy.wait_recv()

        def body(i, carry):
            cols = pl.ds(pl.multiple_of(i * bw, bw), bw)
            up = ownu[s, span, cols].astype(F32) + r2[b, span, cols].astype(F32)
            up = up + bias[:, pl.ds(pl.multiple_of(core * half + i * bw, bw), bw)]
            ownu[s, span, cols] = jax.nn.gelu(up, approximate=True).astype(BF)
            return carry

        lax.fori_loop(0, 6, body, 0)
        send(("own", 1, s, q), [
            Move(ownu.at[s, span], acto.at[b, span], s_core.at[2, b, q], r_core.at[2, b, q], mate)])

    def do_W(b, q):
        s, rows, span = unit(b, q)
        received(acto.at[b, span], r_core.at[2, b, q], s_core.at[2, b, q], mate)
        if (b, q) == (0, 0):
            ready("d")
        scale = guide[b].astype(F32) * 0.25

        def body(i, carry):
            cols = pl.ds(pl.multiple_of(i * tile, tile), tile)
            down = jnp.dot(ownu[s, span], wd[0, :, cols], preferred_element_type=F32)
            down = down + jnp.dot(acto[b, span], wd[1, :, cols], preferred_element_type=F32)
            down = (down * (mod[5, b : b + 1, cols] * scale)).reshape(N, -1, tile)
            acc[:, rows, cols] = down if b == 0 else acc[:, rows, cols] + down
            return carry

        lax.fori_loop(0, width // tile, body, 0, unroll=UNROLL)

    def do_D(t, q):
        rows = part_rows(PARTS[N - 1], q)
        if t == 0:
            settle_reduce(2)
            pb[0, :, rows] = acc[:, rows].astype(BF)
            reduce_start(N, 0, 0, rows, q)
        elif t < N - 1:
            reduce_hop(N, 0, 0, rows, q, t)
        else:
            total = acc[z, rows]
            for b in range(N):
                total = total + (guide[b].astype(F32) * 0.25) * res[b, rows]
            acc[z, rows] = total

            def finish(part):
                acc[z, rows] = acc[z, rows] + part

            reduce_end(N, 0, rows, q, finish)
            out[rows] = acc[z, rows].astype(BF)

    for event in order:
        name, b, p = KINDS[event // 16], event // 4 % 4, event % 4
        if name[0] in "ABC":
            {"A": do_A, "B": do_B, "C": do_C}[name[0]](int(name[1]), b, p)
        elif name[0] == "D":
            do_D(int(name[1]), p)
        elif name in ("U2", "U3"):
            do_U(b, p, int(name[1]) - 2)
        elif name in ("T1", "T2", "O"):
            {"T1": do_T1, "T2": do_T2, "O": do_O}[name](b)
        else:
            {"Q1": do_Q1, "Q2": do_Q2, "N1": do_N1, "N2": do_N2, "U1": do_U1, "G": do_G, "W": do_W}[name](b, p)
    for key in list(pending):
        settle(key)


def fused_layer(clip_tokens, modulation, w_qkv, w_out, w_up, up_bias, w_down, guide_num):
    rows, width = clip_tokens.shape
    chunk = rows // N
    heads = w_qkv.shape[2]
    bw = heads // 4
    half = 6 * bw
    dma, vmem, anywhere = pltpu.SemaphoreType.DMA, pltpu.VMEM, pl.BlockSpec(memory_space=pl.ANY)
    inside = pl.BlockSpec(memory_space=pltpu.VMEM)
    scratch = [
        vmem((N, N, chunk, width), BF),
        vmem((12, width, bw), BF),
        vmem((12, width, bw), BF),
        vmem((heads, width), BF),
        vmem((2, half, width), BF),
        vmem((6, rows, half), BF),
        vmem((N, rows, half), BF),
        vmem((N, rows, half), BF),
        vmem((N, rows, heads), BF),
        vmem((N, rows, half), BF),
        vmem((2, N, chunk, width), BF),
        vmem((N, 2, N - 1, chunk, width), BF),
        vmem((N, chunk, width), F32),
        vmem((N, chunk, width), F32),
        vmem((2, rows, 128), F32),
        vmem((max(rows, 128), 128), F32),
        vmem((N, 8, max(rows, 128)), F32),
        vmem((N, MOST, N, 8, 128), F32),
        dma, dma((12,)), dma((12,)), dma((4,)), dma((2,)),
        dma((3,)), dma((3,)), dma((N, MOST, 3)), dma((N, MOST, 3)),
        dma((2, N, MOST, 2, N - 1)), dma((2, N, MOST, 2, N - 1)),
        dma((N + 1, MOST, 2, N - 1)), dma((N + 1, MOST, 2, N - 1)),
        dma((3, N, MOST)), dma((3, N, MOST)), dma((3, N, MOST)), dma((3, N, MOST)), dma((N, 3)), dma((N, 3)),
    ]
    return pl.pallas_call(
        layer_kernel,
        out_shape=jax.ShapeDtypeStruct((chunk, width), BF),
        in_specs=[anywhere, inside, anywhere, anywhere, anywhere, inside, anywhere,
                  pl.BlockSpec(memory_space=pltpu.SMEM)],
        out_specs=inside,
        scratch_shapes=scratch,
        compiler_params=pltpu.CompilerParams(
            collective_id=0, has_side_effects=True, vmem_limit_bytes=121 * 512 * 1024),
    )(
        clip_tokens, modulation.transpose(1, 0, 2), w_qkv.transpose(1, 0, 2), w_out, w_up,
        up_bias[None], w_down, guide_num,
    )


def on_device(*args):
    tokens, modulation, w_qkv, _, w_up = args[:5]
    head_cols = w_qkv.shape[2]
    square = lax.axis_size("row") == 4 and lax.axis_size("col") == 4 and modulation.shape[0] == 4
    if square and head_cols % 512 == 0 and w_up.shape[1] == 3 * head_cols and tokens.shape[0] % 128 == 0:
        return fused_layer(*args)
    return general_layer(*args)


def solution(mesh):
    in_specs = (
        P(("clips", "col"), "row"),
        P("clips", None, "row"),
        P("row", None, "col"),
        P("col", "row"),
        P("row", "col"),
        P("col"),
        P("col", "row"),
        P("clips"),
    )
    out_specs = P(("clips", "col"), "row")
    return jax.shard_map(
        on_device, mesh=mesh, in_specs=in_specs, out_specs=out_specs, check_vma=False
    )
```

```python
import functools

import jax
import jax.numpy as jnp
from jax import lax
from jax.experimental import pallas as pl
from jax.experimental.pallas import tpu as pltpu
from jax.sharding import PartitionSpec as P

HEAD_DIM = 128
BF = jnp.bfloat16
F32 = jnp.float32
eps = 1e-06
N = 4
IN_PARTS = ((2, 2), (1, 3), (3, 1), (2, 2))
Q_SPLIT = (1, 1, 1, 1)
PARTS = ((2, 2), (2, 2), (2, 2), (2, 2))
MOST = 3
UNROLL = 3
KINDS = (
    "A0", "A1", "A2", "A3", "Q1", "Q2", "T1", "T2", "O", "B1", "B2", "N1", "N2", "C0", "C1", "C2", "C3",
    "U1", "U2", "U3", "G", "W", "D0", "D1", "D2", "D3",
)
ORDER = (
    0, 1, 16, 17, 32, 4, 33, 5, 48, 64, 20, 80, 49, 65, 21, 81, 36, 37, 8, 52,
    68, 9, 96, 53, 84, 12, 69, 24, 85, 13, 112, 128, 40, 25, 144, 28, 100, 56, 72, 41,
    160, 88, 145, 116, 29, 44, 132, 57, 73, 176, 161, 89, 60, 45, 148, 76, 192, 104, 208, 164,
    177, 149, 61, 92, 77, 120, 193, 209, 93, 136, 224, 165, 180, 240, 225, 152, 108, 196, 181, 256,
    212, 272, 241, 153, 288, 124, 168, 197, 304, 213, 257, 140, 273, 228, 169, 184, 289, 305, 156, 244,
    229, 320, 200, 216, 185, 336, 260, 276, 157, 245, 292, 172, 321, 201, 308, 337, 232, 217, 261, 277,
    188, 293, 248, 173, 324, 309, 204, 233, 220, 340, 264, 280, 189, 296, 312, 249, 325, 236, 205, 221,
    341, 265, 281, 252, 297, 237, 328, 313, 268, 344, 284, 300, 316, 253, 329, 345, 269, 285, 301, 332,
    317, 348, 352, 333, 368, 349, 353, 369, 384, 385, 400, 401,
)


def normalize(values, shift, scale):
    totals = lax.psum((jnp.sum(values, axis=1), jnp.sum(values * values, axis=1)), "row")
    width = values.shape[1] * lax.axis_size("row")
    mean = totals[0] / width
    variance = totals[1] / width - mean * mean
    normed = (values - mean[:, None]) * lax.rsqrt(variance + eps)[:, None]
    branches = shift.shape[0]
    shaped = normed.reshape(-1, branches, values.shape[1]) * (1.0 + scale[None]) + shift[None]
    return shaped.reshape(values.shape)


def general_layer(clip_tokens, modulation, w_qkv, w_out, w_up, up_bias, w_down, guide_num):
    branches = modulation.shape[0]
    feat_rows = w_qkv.shape[0]
    head_cols = w_qkv.shape[2]
    heads_here = head_cols // HEAD_DIM
    x_rows = clip_tokens.astype(jnp.float32)
    first = normalize(x_rows, modulation[:, 0], modulation[:, 1]).astype(jnp.bfloat16)
    w_flat = w_qkv.reshape(feat_rows, 3 * head_cols)
    partial_qkv = jnp.dot(
        lax.all_gather(first, "col", axis=0, tiled=True), w_flat, preferred_element_type=jnp.float32
    )
    scale_score = 1.0 / jnp.sqrt(jnp.float32(HEAD_DIM))
    qkv = lax.psum_scatter(partial_qkv.astype(jnp.bfloat16), "row", scatter_dimension=0, tiled=True)
    query3 = qkv[:, :head_cols].reshape(-1, heads_here, HEAD_DIM)
    query_rows = query3.shape[0]
    piece = (
        lax.all_gather(qkv[:, head_cols : 2 * head_cols], "row", axis=0, tiled=True),
        lax.all_gather(qkv[:, 2 * head_cols :], "row", axis=0, tiled=True),
    )
    top = jnp.full((heads_here, query_rows), -1e30, jnp.float32)
    rows = piece[0].shape[0]
    key_heads = piece[0].reshape(rows, heads_here, HEAD_DIM)
    value_heads = piece[1].reshape(rows, heads_here, HEAD_DIM)
    scores = (
        jnp.einsum("qhd,khd->hqk", query3, key_heads, preferred_element_type=jnp.float32)
        * scale_score
    )
    query_branch = jnp.arange(query3.shape[0], dtype=jnp.int32) % branches
    key_branch = jnp.arange(rows, dtype=jnp.int32) % branches
    allowed = (query_branch[:, None] == key_branch[None, :])[None]
    masked = jnp.where(allowed, scores, -1e30)
    new_top = jnp.maximum(top, jnp.max(masked, axis=-1))
    weights = jnp.where(allowed, jnp.exp(masked - new_top[..., None]), 0.0)
    denom = jnp.sum(weights, axis=-1)
    accum = jnp.einsum(
        "hqk,khd->hqd",
        weights.astype(jnp.bfloat16),
        value_heads,
        preferred_element_type=jnp.float32,
    )
    att = (accum / denom[..., None]).transpose(1, 0, 2).reshape(-1, head_cols).astype(jnp.bfloat16)
    partial_out = jnp.dot(
        lax.all_gather(att, "row", axis=0, tiled=True), w_out, preferred_element_type=jnp.float32
    )
    out_rows = lax.psum_scatter(
        partial_out.astype(jnp.bfloat16), "col", scatter_dimension=0, tiled=True
    ).astype(jnp.float32)
    by_branch = x_rows.shape[0] // branches
    resid = (
        x_rows.reshape(by_branch, branches, feat_rows)
        + modulation[None, :, 2] * out_rows.reshape(by_branch, branches, feat_rows)
    ).reshape(x_rows.shape)
    second = normalize(resid, modulation[:, 3], modulation[:, 4]).astype(jnp.bfloat16)
    partial_up = jnp.dot(
        lax.all_gather(second, "col", axis=0, tiled=True), w_up, preferred_element_type=jnp.float32
    )
    up_rows = lax.psum_scatter(
        partial_up.astype(jnp.bfloat16), "row", scatter_dimension=0, tiled=True
    ).astype(jnp.float32)
    act = jax.nn.gelu(up_rows + up_bias[None], approximate=True).astype(jnp.bfloat16)
    partial_down = jnp.dot(
        lax.all_gather(act, "row", axis=0, tiled=True), w_down, preferred_element_type=jnp.float32
    )
    guide_weights = guide_num.astype(jnp.float32) / 4.0
    weights_gate = guide_weights[:, None] * modulation[:, 5]
    combined = jnp.sum(partial_down.reshape(-1, branches, feat_rows) * weights_gate[None], axis=1)
    mlp_rows = lax.psum_scatter(
        combined.astype(jnp.bfloat16), "col", scatter_dimension=0, tiled=True
    ).astype(jnp.float32)
    resid_mix = jnp.sum(
        resid.reshape(by_branch, branches, feat_rows) * guide_weights[None, :, None], axis=1
    )
    return (resid_mix + mlp_rows).astype(jnp.bfloat16)


class Move:
    def __init__(self, src, dst, send, recv, to, sent=None, got=None):
        self.copy = pltpu.make_async_remote_copy(
            src_ref=src, dst_ref=dst, send_sem=send, recv_sem=recv, device_id=to,
            device_id_type=pl.DeviceIdType.MESH,
        )
        self.sent = sent

    def start(self):
        run(self.sent, self.copy.start)

    def wait_send(self):
        run(self.sent, self.copy.wait_send)


def run(cond, act):
    if cond is None:
        act()
    else:
        pl.when(cond)(lambda: act() and None)


def received(dst, recv, send, to):
    pltpu.make_async_remote_copy(
        src_ref=dst, dst_ref=dst, send_sem=send, recv_sem=recv, device_id=to,
        device_id_type=pl.DeviceIdType.MESH,
    ).wait_recv()


def layer_kernel(
    x_hbm, mod, wq_hbm, wo_hbm, wu_hbm, bias, wd_hbm, guide, out,
    xa, wq, wu, wo, wd, work, r1, r2, att, acto, pb, rb, res, acc, xs, st, mom1, mom2,
    lx, lq, lu, lo, ld, s_mom1, r_mom1, s_mom2, r_mom2, s_gat, r_gat, s_red, r_red, s_core, r_core,
    s_x, r_x, s_att, r_att,
):
    r, z = lax.axis_index("row"), lax.axis_index("col")
    core = lax.rem(r, 2)
    chunk, width = xa.shape[2], xa.shape[3]
    sb, ownq, ownu = work.at[0:2], work.at[2:4], work.at[4:6]
    tokens = N * chunk
    bw = wq.shape[2]
    half = 6 * bw
    feats = 4 * width
    tile = 256 if width % 256 == 0 else 128
    mate, across, diag = {"row": r ^ 1}, {"row": r ^ 2}, {"row": r ^ 3}
    above, below = {"col": jnp.minimum(z + 1, N - 1)}, {"col": jnp.maximum(z - 1, 0)}

    local_x = pltpu.make_async_copy(x_hbm, sb.at[0, :, 0:width], lx)
    local_x.start()
    loads = {"q": [], "o": [], "u": [], "d": []}
    for i in (6, 7, 8, 9, 10, 11, 0, 1, 2, 3, 4, 5):
        owner = r ^ (0, 2, 1, 3)[i // 3]
        cols = pl.ds(pl.multiple_of(owner * bw, bw), bw)
        loads["q"].append(pltpu.make_async_copy(wq_hbm.at[i % 3, :, cols], wq.at[i], lq.at[i]))
    for i in range(4):
        owner = r ^ (0, 2, 1, 3)[i]
        rows = pl.ds(pl.multiple_of(owner * bw, bw), bw)
        loads["o"].append(pltpu.make_async_copy(wo_hbm.at[rows], wo.at[pl.ds(i * bw, bw)], lo.at[i]))
    for i in (6, 7, 8, 9, 10, 11, 0, 1, 2, 3, 4, 5):
        side = core if i < 6 else 1 - core
        cols = pl.ds(pl.multiple_of(side * half + (i % 6) * bw, bw), bw)
        loads["u"].append(pltpu.make_async_copy(wu_hbm.at[:, cols], wu.at[i], lu.at[i]))
    for i in range(2):
        side = core if i == 0 else 1 - core
        rows = pl.ds(pl.multiple_of(side * half, bw), half)
        loads["d"].append(pltpu.make_async_copy(wd_hbm.at[rows], wd.at[i], ld.at[i]))

    def ready(name, only=None):
        for i, load in enumerate(loads[name]):
            if only is None or i in only:
                load.wait()

    barrier = pltpu.get_barrier_semaphore()

    def greet(to, cond=None):
        run(cond, lambda: pl.semaphore_signal(barrier, inc=1, device_id=to, device_id_type=pl.DeviceIdType.MESH))

    for to in (mate, across, diag):
        greet(to)
    greet(above, z < N - 1)
    greet(below, z > 0)
    inner = (z > 0) & (z < N - 1)
    run(inner, lambda: pl.semaphore_wait(barrier, 5))
    run(jnp.logical_not(inner), lambda: pl.semaphore_wait(barrier, 4))

    local_x.wait()
    for group in loads.values():
        for load in group:
            load.start()

    pending = {}

    def send(key, moves):
        pending[key] = moves
        for move in moves:
            move.start()

    def settle(key):
        for move in pending.pop(key, []):
            move.wait_send()

    def stats_rows(values, into, rows):
        total = jnp.sum(values, axis=1, keepdims=True)
        squares = jnp.sum(values * values, axis=1, keepdims=True)
        lane = lax.broadcasted_iota(jnp.int32, (values.shape[0], 128), 1)
        into[rows, :] = jnp.where(lane == 0, total, squares)

    def scales(total):
        mean = total[0:1] / feats
        rstd = lax.rsqrt(total[1:2] / feats - mean * mean + eps)
        lane = lax.broadcasted_iota(jnp.int32, (128, total.shape[1]), 0)
        return jnp.where(lane == 0, mean, rstd).T

    for i in range(width // 128):
        cols = slice(i * 128, (i + 1) * 128)
        xs[i % 2] = sb[0, :, cols].astype(F32)
        for b in range(N):
            res[b, :, cols] = xs[i % 2, pl.ds(b, chunk, stride=N), :]
    for b in range(N):
        stats_rows(res[b], st, slice(b * chunk, (b + 1) * chunk))
    mom1[0] = st[...].T[0:8]
    send("mom1", [
        Move(mom1.at[0], mom1.at[m], s_mom1.at[m - 1], r_mom1.at[m - 1], to)
        for m, to in ((1, mate), (2, across), (3, diag))
    ])
    for m in (1, 2, 3):
        received(mom1.at[m], r_mom1.at[m - 1], s_mom1.at[m - 1], mate)
    st[...] = scales(mom1[0] + mom1[1] + mom1[2] + mom1[3])

    def part_rows(sizes, p, whole=chunk):
        return slice(sum(sizes[:p]) * (whole // 4), sum(sizes[: p + 1]) * (whole // 4))

    gather_sizes = (IN_PARTS, PARTS)

    def gather_start(stage, b, p):
        mine = xa.at[b, z, part_rows(gather_sizes[stage][b], p)]
        sends, gets = s_gat.at[stage, b, p], r_gat.at[stage, b, p]
        up = Move(mine, mine, sends.at[0, 0], gets.at[0, 0], above, z < N - 1)
        down = Move(mine, mine, sends.at[1, 0], gets.at[1, 0], below, z > 0)
        send(("gat", stage, b, p, 0), [up, down])

    def gather_hop(stage, b, p, h):
        low, high = jnp.maximum(z - h, 0), jnp.minimum(z + h, N - 1)
        rows = part_rows(gather_sizes[stage][b], p)
        sends, gets = s_gat.at[stage, b, p], r_gat.at[stage, b, p]
        moves = []

        def hop(side, at, here, on, to):
            data = xa.at[b, at, rows]
            run(here, lambda: received(data, gets.at[side, h - 1], sends.at[side, 0], to))
            if h < N - 1:
                move = Move(data, data, sends.at[side, h], gets.at[side, h], to, here & on)
                move.start()
                moves.append(move)

        hop(0, low, z >= h, z < N - 1, above)
        hop(1, high, z + h <= N - 1, z > 0, below)
        pending[("gat", stage, b, p, h)] = moves

    def settle_gather(stage, b):
        for p in range(len(gather_sizes[stage][b])):
            for h in range(N):
                settle(("gat", stage, b, p, h))

    def red_move(b, key, slot, rows, p, side, j):
        k = j if side == 0 else N - 1 - j
        to = below if side == 0 else above
        return pb.at[slot, k, rows], rb.at[key, side, j, rows], s_red.at[b, p, side, j], r_red.at[b, p, side, j], to

    def reduce_start(b, key, slot, rows, p):
        moves = []
        for j in range(N - 1):
            moves.append(Move(*red_move(b, key, slot, rows, p, 0, j), z == N - 1))
            moves.append(Move(*red_move(b, key, slot, rows, p, 1, j), z == 0))
        send(("red", b, p, 0), moves)

    def reduce_hop(b, key, slot, rows, p, t):
        moves = []

        def hop(side, j, valid):
            j = jnp.clip(j, 0, N - 2)
            src, dst, ss, rs, to = red_move(b, key, slot, rows, p, side, j)

            @pl.when(valid)
            def _():
                received(dst, rs, ss, to)
                k = j if side == 0 else N - 1 - j
                pb[slot, k, rows] = (pb[slot, k, rows].astype(F32) + rb[key, side, j, rows].astype(F32)).astype(BF)

            move = Move(src, dst, ss, rs, to, valid)
            move.start()
            moves.append(move)

        down, up = t - (N - 1 - z), t - z
        hop(0, down, (z < N - 1) & (down >= 0) & (down < z))
        hop(1, up, (z > 0) & (up >= 0) & (up < N - 1 - z))
        pending[("red", b, p, t)] = moves

    def reduce_end(b, key, rows, p, add):
        for side, j, valid in ((0, z, z < N - 1), (1, N - 1 - z, z > 0)):
            j = jnp.minimum(j, N - 2)

            def take(side=side, j=j):
                received(rb.at[key, side, j, rows], r_red.at[b, p, side, j], s_red.at[b, p, side, j], mate)
                add(rb[key, side, j, rows].astype(F32))

            run(valid, take)

    def settle_reduce(b):
        for p in range(MOST):
            for t in range(N - 1):
                settle(("red", b, p, t))

    order = list(ORDER)
    for b in range(N):
        sc = st[b * chunk : (b + 1) * chunk, :]
        normed = (res[b] - sc[:, 0:1]) * sc[:, 1:2]
        xa[b, z] = (normed * (1.0 + mod[1, b : b + 1, :]) + mod[0, b : b + 1, :]).astype(BF)
        while order[0] < 16 and order[0] // 4 == b:
            gather_start(0, b, order.pop(0) % 4)

    def project_all(kind, b, p, rows, span, s, weight, name):
        settle(("core", s))
        if (b, p) == (0, 0):
            ready(name)
        for old in range(MOST):
            if p == 0 or kind:
                settle(("own", kind, s, old))
        away = Move(sb.at[s, span], r1.at[b, span], s_core.at[kind, b, p], r_core.at[kind, b, p], mate)

        def body(g, carry):
            pl.when(g == 1)(lambda: away.start())
            slot = jnp.where(g == 0, s, 2 + 2 * kind + s)
            left = xa[b, :, rows].reshape(-1, width)
            for k in range(6):
                part = jnp.dot(left, weight[6 * (1 - g) + k], preferred_element_type=F32)
                work[slot, span, k * bw : (k + 1) * bw] = part.astype(BF)
            return carry

        lax.fori_loop(0, 2, body, 0)
        pending[("core", s)] = [away]

    def pair_sum(own, s, b, span, cols):
        own[s, span, cols] = (own[s, span, cols].astype(F32) + r1[b, span, cols].astype(F32)).astype(BF)

    def do_A(h, b, p):
        if h == 0:
            gather_start(0, b, p)
        else:
            gather_hop(0, b, p, h)

    def q_parts(b):
        if not Q_SPLIT[b]:
            return [(slice(0, chunk), slice(0, tokens))]
        sizes = IN_PARTS[b]
        return [(part_rows(sizes, p), part_rows(sizes, p, tokens)) for p in range(len(sizes))]

    def do_Q1(b, p):
        rows, span = q_parts(b)[p]
        project_all(0, b, p, rows, span, b % 2, wq, "q")

    def q_move(b, p):
        span = q_parts(b)[p][1]
        return Move(
            ownq.at[b % 2, span, 3 * bw : half], r2.at[b, span, 0 : 3 * bw], s_x.at[0, b, p], r_x.at[0, b, p], across)

    def do_Q2(b, p):
        span = q_parts(b)[p][1]
        received(r1.at[b, span], r_core.at[0, b, p], s_core.at[0, b, p], mate)
        for i in range(3, 6):
            pair_sum(ownq, b % 2, b, span, slice(i * bw, (i + 1) * bw))
        send(("own", 0, b % 2, p), [q_move(b, p)])

    def do_T1(b):
        for p, (_, span) in enumerate(q_parts(b)):
            received(r2.at[b, span, 0 : 3 * bw], r_x.at[0, b, p], s_x.at[0, b, p], across)
        qkv = []
        for j in range(3):
            cols = slice(j * bw, (j + 1) * bw)
            total = ownq[b % 2, :, cols].astype(F32) + r1[b, :, cols].astype(F32) + r2[b, :, cols].astype(F32)
            qkv.append(total.astype(BF))
        for h in range(bw // HEAD_DIM):
            cols = slice(h * HEAD_DIM, (h + 1) * HEAD_DIM)
            scores = lax.dot_general(
                qkv[0][:, cols], qkv[1][:, cols], (((1,), (1,)), ((), ())), preferred_element_type=F32)
            scores = scores * (1.0 / HEAD_DIM**0.5)
            weights = jnp.exp(scores - jnp.max(scores, axis=-1, keepdims=True))
            denom = jnp.sum(weights, axis=-1, keepdims=True)
            mixed = jnp.dot(weights.astype(BF), qkv[2][:, cols], preferred_element_type=F32)
            att[b, :, cols] = (mixed / denom).astype(BF)
        send(("att", b, 0), [
            Move(att.at[b, :, 0:bw], att.at[b, :, bw : 2 * bw], s_att.at[b, 0], r_att.at[b, 0], across),
            Move(att.at[b, :, 0:bw], att.at[b, :, 2 * bw : 3 * bw], s_att.at[b, 1], r_att.at[b, 1], mate),
        ])

    def do_T2(b):
        received(att.at[b, :, bw : 2 * bw], r_att.at[b, 0], s_att.at[b, 0], across)
        send(("att", b, 1), [
            Move(att.at[b, :, bw : 2 * bw], att.at[b, :, 3 * bw : 4 * bw], s_att.at[b, 2], r_att.at[b, 2], mate)])

    def do_O(b):
        received(att.at[b, :, 2 * bw : 3 * bw], r_att.at[b, 1], s_att.at[b, 1], mate)
        received(att.at[b, :, 3 * bw : 4 * bw], r_att.at[b, 2], s_att.at[b, 2], mate)
        if b == 0:
            ready("o")
        if b >= 2:
            settle_reduce(b - 2)
        settle_gather(0, b)

        def body(i, carry):
            cols = pl.ds(pl.multiple_of(i * tile, tile), tile)
            part = jnp.dot(att[b], wo[:, cols], preferred_element_type=F32).astype(BF)
            for rows, span in q_parts(b):
                pb[b % 2, :, rows, cols] = part[span].reshape(N, -1, tile)
            return carry

        lax.fori_loop(0, width // tile, body, 0, unroll=UNROLL)
        for p in range(len(PARTS[b])):
            reduce_start(b, b, b % 2, part_rows(PARTS[b], p), p)

    def do_B(t, b, p):
        reduce_hop(b, b, b % 2, part_rows(PARTS[b], p), p, t)

    def do_N1(b, p):
        gate, rows = mod[2, b : b + 1, :], part_rows(PARTS[b], p)
        res[b, rows] = res[b, rows] + gate * pb[b % 2, z, rows].astype(F32)

        def add(part):
            res[b, rows] = res[b, rows] + gate * part

        reduce_end(b, b, rows, p, add)
        stats_rows(res[b, rows], st, slice(0, rows.stop - rows.start))
        mom2[b, p, 0] = st[0:128, :].T[0:8]
        send(("mom2", b, p), [
            Move(mom2.at[b, p, 0], mom2.at[b, p, m], s_mom2.at[b, p, m - 1], r_mom2.at[b, p, m - 1], to)
            for m, to in ((1, mate), (2, across), (3, diag))
        ])

    def do_N2(b, p):
        rows = part_rows(PARTS[b], p)
        for m in (1, 2, 3):
            received(mom2.at[b, p, m], r_mom2.at[b, p, m - 1], s_mom2.at[b, p, m - 1], mate)
        total = mom2[b, p, 0] + mom2[b, p, 1] + mom2[b, p, 2] + mom2[b, p, 3]
        sc = scales(total)[0 : rows.stop - rows.start]
        normed = (res[b, rows] - sc[:, 0:1]) * sc[:, 1:2]
        xa[b, z, rows] = (normed * (1.0 + mod[4, b : b + 1, :]) + mod[3, b : b + 1, :]).astype(BF)

    def do_C(h, b, p):
        if h == 0:
            gather_start(1, b, p)
        else:
            gather_hop(1, b, p, h)

    units = [(b, q) for b in range(N) for q in range(len(PARTS[b]))]

    def unit(b, q):
        return units.index((b, q)) % 2, part_rows(PARTS[b], q), part_rows(PARTS[b], q, tokens)

    def do_U1(b, q):
        s, rows, span = unit(b, q)
        project_all(1, b, q, rows, span, s, wu, "u")

    def up_move(b, q, part):
        s, _, span = unit(b, q)
        cols = slice(part * 3 * bw, (part + 1) * 3 * bw)
        sem = 1 + part
        return Move(ownu.at[s, span, cols], r2.at[b, span, cols], s_x.at[sem, b, q], r_x.at[sem, b, q], across)

    def do_U(b, q, part):
        s, _, span = unit(b, q)
        if part == 0:
            received(r1.at[b, span], r_core.at[1, b, q], s_core.at[1, b, q], mate)
        for i in range(3 * part, 3 * part + 3):
            pair_sum(ownu, s, b, span, slice(i * bw, (i + 1) * bw))
        send(("ux", b, q, part), [up_move(b, q, part)])

    def do_G(b, q):
        s, _, span = unit(b, q)
        for part in range(2):
            settle(("ux", b, q, part))
            up_move(b, q, part).copy.wait_recv()

        def body(i, carry):
            cols = pl.ds(pl.multiple_of(i * bw, bw), bw)
            up = ownu[s, span, cols].astype(F32) + r2[b, span, cols].astype(F32)
            up = up + bias[:, pl.ds(pl.multiple_of(core * half + i * bw, bw), bw)]
            ownu[s, span, cols] = jax.nn.gelu(up, approximate=True).astype(BF)
            return carry

        lax.fori_loop(0, 6, body, 0)
        send(("own", 1, s, q), [
            Move(ownu.at[s, span], acto.at[b, span], s_core.at[2, b, q], r_core.at[2, b, q], mate)])

    def do_W(b, q):
        s, rows, span = unit(b, q)
        received(acto.at[b, span], r_core.at[2, b, q], s_core.at[2, b, q], mate)
        if (b, q) == (0, 0):
            ready("d")
        scale = guide[b].astype(F32) * 0.25

        def body(i, carry):
            cols = pl.ds(pl.multiple_of(i * tile, tile), tile)
            down = jnp.dot(ownu[s, span], wd[0, :, cols], preferred_element_type=F32)
            down = down + jnp.dot(acto[b, span], wd[1, :, cols], preferred_element_type=F32)
            down = (down * (mod[5, b : b + 1, cols] * scale)).reshape(N, -1, tile)
            acc[:, rows, cols] = down if b == 0 else acc[:, rows, cols] + down
            return carry

        lax.fori_loop(0, width // tile, body, 0, unroll=UNROLL)

    def do_D(t, q):
        rows = part_rows(PARTS[N - 1], q)
        if t == 0:
            settle_reduce(2)
            pb[0, :, rows] = acc[:, rows].astype(BF)
            reduce_start(N, 0, 0, rows, q)
        elif t < N - 1:
            reduce_hop(N, 0, 0, rows, q, t)
        else:
            total = acc[z, rows]
            for b in range(N):
                total = total + (guide[b].astype(F32) * 0.25) * res[b, rows]
            acc[z, rows] = total

            def finish(part):
                acc[z, rows] = acc[z, rows] + part

            reduce_end(N, 0, rows, q, finish)
            out[rows] = acc[z, rows].astype(BF)

    for event in order:
        name, b, p = KINDS[event // 16], event // 4 % 4, event % 4
        if name[0] in "ABC":
            {"A": do_A, "B": do_B, "C": do_C}[name[0]](int(name[1]), b, p)
        elif name[0] == "D":
            do_D(int(name[1]), p)
        elif name in ("U2", "U3"):
            do_U(b, p, int(name[1]) - 2)
        elif name in ("T1", "T2", "O"):
            {"T1": do_T1, "T2": do_T2, "O": do_O}[name](b)
        else:
            {"Q1": do_Q1, "Q2": do_Q2, "N1": do_N1, "N2": do_N2, "U1": do_U1, "G": do_G, "W": do_W}[name](b, p)
    for key in list(pending):
        settle(key)


def fused_layer(clip_tokens, modulation, w_qkv, w_out, w_up, up_bias, w_down, guide_num):
    rows, width = clip_tokens.shape
    chunk = rows // N
    heads = w_qkv.shape[2]
    bw = heads // 4
    half = 6 * bw
    dma, vmem, anywhere = pltpu.SemaphoreType.DMA, pltpu.VMEM, pl.BlockSpec(memory_space=pl.ANY)
    inside = pl.BlockSpec(memory_space=pltpu.VMEM)
    scratch = [
        vmem((N, N, chunk, width), BF),
        vmem((12, width, bw), BF),
        vmem((12, width, bw), BF),
        vmem((heads, width), BF),
        vmem((2, half, width), BF),
        vmem((6, rows, half), BF),
        vmem((N, rows, half), BF),
        vmem((N, rows, half), BF),
        vmem((N, rows, heads), BF),
        vmem((N, rows, half), BF),
        vmem((2, N, chunk, width), BF),
        vmem((N, 2, N - 1, chunk, width), BF),
        vmem((N, chunk, width), F32),
        vmem((N, chunk, width), F32),
        vmem((2, rows, 128), F32),
        vmem((max(rows, 128), 128), F32),
        vmem((N, 8, max(rows, 128)), F32),
        vmem((N, MOST, N, 8, 128), F32),
        dma, dma((12,)), dma((12,)), dma((4,)), dma((2,)),
        dma((3,)), dma((3,)), dma((N, MOST, 3)), dma((N, MOST, 3)),
        dma((2, N, MOST, 2, N - 1)), dma((2, N, MOST, 2, N - 1)),
        dma((N + 1, MOST, 2, N - 1)), dma((N + 1, MOST, 2, N - 1)),
        dma((3, N, MOST)), dma((3, N, MOST)), dma((3, N, MOST)), dma((3, N, MOST)), dma((N, 3)), dma((N, 3)),
    ]
    return pl.pallas_call(
        layer_kernel,
        out_shape=jax.ShapeDtypeStruct((chunk, width), BF),
        in_specs=[anywhere, inside, anywhere, anywhere, anywhere, inside, anywhere,
                  pl.BlockSpec(memory_space=pltpu.SMEM)],
        out_specs=inside,
        scratch_shapes=scratch,
        compiler_params=pltpu.CompilerParams(
            collective_id=0, has_side_effects=True, vmem_limit_bytes=121 * 512 * 1024),
    )(
        clip_tokens, modulation.transpose(1, 0, 2), w_qkv.transpose(1, 0, 2), w_out, w_up,
        up_bias[None], w_down, guide_num,
    )


def on_device(*args):
    tokens, modulation, w_qkv, _, w_up = args[:5]
    head_cols = w_qkv.shape[2]
    square = lax.axis_size("row") == 4 and lax.axis_size("col") == 4 and modulation.shape[0] == 4
    if square and head_cols % 512 == 0 and w_up.shape[1] == 3 * head_cols and tokens.shape[0] % 128 == 0:
        return fused_layer(*args)
    return general_layer(*args)


def solution(mesh):
    in_specs = (
        P(("clips", "col"), "row"),
        P("clips", None, "row"),
        P("row", None, "col"),
        P("col", "row"),
        P("row", "col"),
        P("col"),
        P("col", "row"),
        P("clips"),
    )
    out_specs = P(("clips", "col"), "row")
    return jax.shard_map(
        on_device, mesh=mesh, in_specs=in_specs, out_specs=out_specs, check_vma=False
    )
```
